128 devices in a mesh: req: 32 (over z, x, core), tp: 4 (over y).
Axes of the slice: x: 4, y: 4, z: 4, core: 2. Of those that a mesh axis runs over, the one named last changes fastest.
Arguments:
- tokens: bfloat16 [12288, 5120], P('req'), may hold values from -40 to 40
- w_query: bfloat16 [5120, 2560], P(None, 'tp'), may hold values from -0.125 to 0.125
- query_bias: float32 [2560], P('tp'), may hold values from -24 to 24
- w_keyval: bfloat16 [5120, 1024], P(None, 'tp'), may hold values from -0.21875 to 0.21875
- keyval_bias: float32 [1024], P('tp'), may hold values from -2.5 to 2.5
- w_out: bfloat16 [2560, 5120], P('tp'), may hold values from -0.25 to 0.25
- attn_gain: float32 [5120], replicated, may hold values from 0.25 to 1.75
- final_norm_gain: float32 [5120], replicated, may hold values from 0.25 to 1.75
- head_weight: bfloat16 [5120, 76032], P(None, ('req', 'tp')), may hold values from -0.25 to 0.25
- kv_pool: bfloat16 [851968, 4, 256], P('req', 'tp'), may hold values from -17 to 17
- cache_len: int32 [512], replicated, may hold values from 256 to 3072, as said below
Outputs:
- states: bfloat16 [12288, 5120], P('req', 'tp')
- new_kv: bfloat16 [12288, 4, 256], P('req', 'tp')
- row_norms: float32 [512], P('req')
- logit_max: float32 [512], replicated
- logits: float32 [512, 76032], P(None, ('req', 'tp'))
The draws below stay inside these ranges and needn't reach their ends.
Inputs may be any that keep to these rules, and one draw needn't show every extreme that they name: `cache_len`: every cache holds 256 or 3072 rows. Exactly 64 requests hold 3072; requests i * 16 to i * 16 + 15 hold at most 8 of them for every i, and exactly 8 for some i, so their caches fill at most 26624 rows, and exactly 26624 for some i.
All inputs are finite; a program needn't handle non-finite values.
Results may differ from the reference program's by a relative error of at most 0.014.
Values may be sent and summed in bfloat16 or wider, within the bound.
A program may use at most 192 MiB of HBM per device.

```python
import math
import jax
import jax.numpy as jnp
from jax import lax

D = 5120
HD = 128
KVH = 4
GROUP = 5
VOCAB = 76032
NEW = 24
SHORT = 256
LONG = 3072
REQ_DEV = 16
HEADS = 20
LMAX = 8
POOL = 26624
REQUESTS = 512
LONGS = 64
TOKENS = 12288
N_REQ = 32


def draw_tokens(key, part):
    token_count = REQUESTS * NEW
    columns = jnp.arange(D, dtype=jnp.float32)
    rising = 0.75 * jnp.exp(0.5 * math.log(3.0) / (D - 1) * columns)
    base = jnp.clip(jax.random.normal(key, (token_count, D), jnp.float32), -5.0, 5.0)
    return (base * rising[None, :]).astype(jnp.bfloat16)


def draw_query_bias(key, part):
    return jnp.clip(0.5 * jax.random.normal(key, (KVH * GROUP * HD,), jnp.float32), -2.0, 2.0)


def draw_kv_pool(key, part):
    total_rows = N_REQ * POOL
    return jnp.clip(jax.random.normal(key, (total_rows, KVH, 2 * HD), jnp.float32), -4.0, 4.0).astype(jnp.bfloat16)


def draw_cache_len(key, part):
    heavy = max(1, LONGS // (2 * LMAX))
    spare = N_REQ - heavy
    leftover = LONGS - heavy * LMAX
    device_order = jax.random.permutation(jax.random.fold_in(key, 11), N_REQ)
    device_rank = jnp.argsort(device_order).astype(jnp.int32)
    spread_count = (leftover + device_rank - heavy) // spare
    counts = jnp.where(device_rank < heavy, LMAX, spread_count).astype(jnp.int32)
    raw_scores = jax.random.randint(jax.random.fold_in(key, 12), (N_REQ, REQ_DEV), 0, 1 << 20, jnp.int32)
    slot_scores = raw_scores * REQ_DEV + jnp.arange(REQ_DEV, dtype=jnp.int32)[None, :]
    slot_order = jnp.argsort(slot_scores, axis=1)
    slot_rank = jnp.argsort(slot_order, axis=1).astype(jnp.int32)
    lengths = jnp.where(slot_rank < counts[:, None], LONG, SHORT)
    return lengths.reshape(-1).astype(jnp.int32)


def levels(key, shape, split, least, high):
    def one(dim, parts):
        heights = jax.random.uniform(jax.random.fold_in(jax.random.fold_in(key, 6), dim), (parts,), jnp.float32, least / len(split), high / len(split))
        return jnp.repeat(jnp.exp(heights), shape[dim] // parts).reshape((-1,) + (1,) * (len(shape) - dim - 1))

    gain = one(*split[0])
    for cut in split[1:]:
        gain = gain * one(*cut)
    return gain


def bell_draw(key, shape, width, reach, shards=(), kind=jnp.bfloat16):
    values = width * jax.random.normal(key, shape, jnp.float32)
    if shards:
        values = values * levels(key, shape, shards, -0.22, 0.18)
    return jnp.clip(values, -reach, reach).astype(kind)


def setup_inputs(seed: int = 0) -> dict:
    key_of = jax.random.split(jax.random.key(seed), 12)
    return {
        "tokens": draw_tokens(jax.random.fold_in(key_of[11], 71), 0),
        "w_query": bell_draw(key_of[1], (D, HEADS * HD), (D // 2) ** -0.5, 0.125, ((1, 4),)),
        "query_bias": draw_query_bias(jax.random.fold_in(key_of[11], 71), 0),
        "w_keyval": bell_draw(key_of[3], (D, 2 * KVH * HD), (D // 6) ** -0.5, 0.21875, ((1, 4),)),
        "keyval_bias": bell_draw(key_of[4], (2 * KVH * HD,), 0.5, 2.5, ((0, 4),), jnp.float32),
        "w_out": bell_draw(key_of[5], (HEADS * HD, D), (HEADS * HD // 4) ** -0.5, 0.25, ((0, 4),)),
        "attn_gain": jnp.clip(1.0 + 0.15 * jax.random.normal(key_of[6], (D,), jnp.float32), 0.25, 1.75),
        "final_norm_gain": jnp.clip(1.0 + 0.15 * jax.random.normal(key_of[7], (D,), jnp.float32), 0.25, 1.75),
        "head_weight": bell_draw(key_of[8], (D, VOCAB), (D // 9) ** -0.5, 0.25, ((1, 128),)),
        "kv_pool": draw_kv_pool(jax.random.fold_in(key_of[11], 71), 0),
        "cache_len": draw_cache_len(jax.random.fold_in(key_of[11], 71), 0),
    }


THETA = 1000000.0
EPS = 1e-06

def rope_rotate(vectors, positions):
    head_width = vectors.shape[-1]
    halfway = head_width // 2
    frequency = THETA ** (-(jnp.arange(halfway, dtype=jnp.float32) * (2.0 / head_width)))
    angles = positions[..., None] * frequency
    cosine = jnp.cos(angles)
    sine_part = jnp.sin(angles)
    front_part = vectors[..., :halfway]
    back_part = vectors[..., halfway:]
    return jnp.concatenate([front_part * cosine - back_part * sine_part, back_part * cosine + front_part * sine_part], axis=-1)

def attend_one(q_req, k_req, v_req, row_begin, length, kv_pool):
    total_rows = kv_pool.shape[0]
    row_first = jnp.minimum(row_begin, total_rows - LONG).astype(jnp.int32)
    window = lax.dynamic_slice_in_dim(kv_pool, row_first, LONG, 0)
    row_index = row_first + jnp.arange(LONG, dtype=jnp.int32)
    inside = (row_index >= row_begin) & (row_index < row_begin + length)
    query_f = q_req.astype(jnp.float32)
    cache_scores = jnp.einsum('nkgd,lkd->kgnl', query_f, window[..., :HD].astype(jnp.float32))
    cache_scores = jnp.where(inside[None, None, None, :], cache_scores, -jnp.inf)
    new_scores = jnp.einsum('nkgd,mkd->kgnm', query_f, k_req.astype(jnp.float32))
    causal = jnp.arange(NEW, dtype=jnp.int32)[:, None] >= jnp.arange(NEW, dtype=jnp.int32)[None, :]
    new_scores = jnp.where(causal[None, None], new_scores, -jnp.inf)
    scores = jnp.concatenate([cache_scores, new_scores], axis=-1)
    row_max = lax.optimization_barrier(jnp.max(scores, axis=-1, keepdims=True))
    exps = jnp.exp(scores - row_max)
    totals = lax.optimization_barrier(jnp.sum(exps, axis=-1))
    rounded = lax.optimization_barrier(exps.astype(jnp.bfloat16)).astype(jnp.float32)
    value_matrix = jnp.concatenate([window[..., HD:], v_req], axis=0).astype(jnp.float32)
    mixed = jnp.einsum('kgnl,lkd->nkgd', rounded, value_matrix)
    return (mixed / jnp.transpose(totals, (2, 0, 1))[..., None]).astype(jnp.bfloat16)

def reference(tokens, w_query, query_bias, w_keyval, keyval_bias, w_out, attn_gain, final_norm_gain, head_weight, kv_pool, cache_len):
    source = tokens.astype(jnp.float32)
    mean_square = lax.optimization_barrier(jnp.mean(source * source, axis=1, keepdims=True))
    normed = (source / jnp.sqrt(mean_square + EPS) * attn_gain[None, :]).astype(jnp.bfloat16)
    query_raw = jnp.dot(normed, w_query, preferred_element_type=jnp.float32) + query_bias[None, :]
    keyval_raw = jnp.dot(normed, w_keyval, preferred_element_type=jnp.float32) + keyval_bias[None, :]
    positions = (cache_len[:, None] + jnp.arange(NEW, dtype=jnp.int32)[None, :]).astype(jnp.float32)
    query_heads = query_raw.reshape(REQUESTS, NEW, KVH, GROUP, HD)
    queries = (rope_rotate(query_heads, positions[:, :, None, None]) * (1.0 / math.sqrt(HD))).astype(jnp.bfloat16)
    keyval_heads = keyval_raw.reshape(REQUESTS, NEW, KVH, 2, HD)
    key_new = rope_rotate(keyval_heads[:, :, :, 0, :], positions[:, :, None]).astype(jnp.bfloat16)
    value_new = keyval_heads[:, :, :, 1, :].astype(jnp.bfloat16)
    new_kv = jnp.concatenate([key_new, value_new], axis=-1).reshape(TOKENS, KVH, 2 * HD)
    lens_grid = cache_len.reshape(N_REQ, REQ_DEV)
    row_starts = (jnp.arange(N_REQ, dtype=jnp.int32)[:, None] * POOL + jnp.cumsum(lens_grid, axis=1) - lens_grid).reshape(-1).astype(jnp.int32)

    def one_request(inputs):
        q_req, k_req, v_req, row_begin, length = inputs
        return attend_one(q_req, k_req, v_req, row_begin, length, kv_pool)
    mixed = lax.map(one_request, (queries, key_new, value_new, row_starts, cache_len.astype(jnp.int32)))
    attention = mixed.reshape(TOKENS, HEADS * HD)
    projected = jnp.dot(attention, w_out, preferred_element_type=jnp.float32)
    states = (source + projected).astype(jnp.bfloat16)
    last_rows = states.reshape(REQUESTS, NEW, D)[:, NEW - 1, :].astype(jnp.float32)
    row_norms = jnp.sqrt(lax.optimization_barrier(jnp.mean(last_rows * last_rows, axis=1)) + EPS)
    final_rows = (last_rows / row_norms[:, None] * final_norm_gain[None, :]).astype(jnp.bfloat16)
    logits = jnp.dot(final_rows, head_weight, preferred_element_type=jnp.float32)
    logit_max = lax.optimization_barrier(jnp.max(logits, axis=1))
    return (states, new_kv, row_norms, logit_max, logits)
```

```python
import math

import jax
import jax.numpy as jnp
import numpy as np
from jax import lax
from jax.experimental import pallas as pl
from jax.experimental.pallas import tpu as pltpu
from jax.sharding import PartitionSpec as P

D = 5120
HD = 128
GROUP = 5
NEW = 24
SHORT = 256
LONG = 3072
REQ_DEV = 16
POOL = 26624
ROWS = REQ_DEV * NEW
QW = GROUP * HD
KW = 2 * HD
THETA = 1000000.0
EPS = 1e-06
NEG = -1e30

KC = 1024
NKC = D // KC
PC = 2048
NPC = POOL // PC
QR = 128


def rope_tables():
    freq = np.float32(THETA) ** (-(np.arange(HD // 2, dtype=np.float32) * np.float32(2.0 / HD)))
    pos = np.concatenate([SHORT + np.arange(NEW), LONG + np.arange(NEW)]).astype(np.float32)
    ang = (pos[:, None] * freq[None, :].astype(np.float32)).astype(np.float64)
    cos = np.cos(ang).astype(np.float32)
    sin = np.sin(ang).astype(np.float32)
    return np.concatenate([cos, cos, -sin, sin], axis=1)


def attn_kernel(
    lens_ref,
    tok_hbm,
    wq_hbm,
    wkv_hbm,
    qb_ref,
    kvb_ref,
    gain_ref,
    cs_ref,
    pool_hbm,
    newkv_ref,
    attn_ref,
    last_ref,
    tok_v,
    w_v,
    pool_v,
    acc,
    ss,
    tok_sem,
    wq_sem,
    wkv_sem,
    pool_sem,
):
    def tok_copy(k):
        c = pl.ds(pl.multiple_of(k * KC, KC), KC)
        return pltpu.make_async_copy(tok_hbm.at[:, c], tok_v.at[:, c], tok_sem.at[k])

    def wq_copy(k):
        c = pl.ds(pl.multiple_of(k * KC, KC), KC)
        return pltpu.make_async_copy(wq_hbm.at[c, :], w_v.at[c, pl.ds(0, QW)], wq_sem.at[k])

    def wkv_copy(k):
        c = pl.ds(pl.multiple_of(k * KC, KC), KC)
        return pltpu.make_async_copy(wkv_hbm.at[c, :], w_v.at[c, pl.ds(QW, KW)], wkv_sem.at[k])

    def pool_copy(k):
        c = pl.ds(pl.multiple_of(k * PC, PC), PC)
        return pltpu.make_async_copy(pool_hbm.at[c, :], pool_v.at[c, :], pool_sem.at[k])

    for k in range(NKC):
        tok_copy(k).start()
        wq_copy(k).start()
        wkv_copy(k).start()
    for k in range(NPC):
        pool_copy(k).start()

    ss[...] = jnp.zeros_like(ss)
    acc[...] = jnp.zeros_like(acc)

    @pl.loop(0, NKC)
    def _(k):
        tok_copy(k).wait()
        wq_copy(k).wait()
        wkv_copy(k).wait()
        c = pl.ds(pl.multiple_of(k * KC, KC), KC)
        x = tok_v[:, c].astype(jnp.float32)
        sq = x * x
        part = sq[:, 0:HD]
        for i in range(1, KC // HD):
            part = part + sq[:, i * HD : (i + 1) * HD]
        ss[...] += part
        xg = (x * gain_ref[:, c]).astype(jnp.bfloat16)
        acc[...] += jnp.dot(xg, w_v[c, :], preferred_element_type=jnp.float32)

    rstd = 1.0 / jnp.sqrt(jnp.sum(ss[...], axis=1, keepdims=True) * (1.0 / D) + EPS)
    ss[...] = jnp.broadcast_to(rstd, ss.shape)

    row = lax.broadcasted_iota(jnp.int32, (QR, HD), 0)
    col = lax.broadcasted_iota(jnp.int32, (QR, HD), 1)
    token = row
    for g in range(1, GROUP + 1):
        token = token - jnp.where(row >= g * NEW, NEW, 0)
    causal = (col <= token) & (col < NEW)
    base = lax.axis_index("req") * REQ_DEV
    scale = 1.0 / math.sqrt(HD)

    def request(r, carry):
        begin, waited = carry
        length = lens_ref[base + r]
        is_long = length > SHORT
        need = (begin + length + (PC - 1)) // PC

        def wait_one(i, c):
            pool_copy(i).wait()
            return c

        lax.fori_loop(waited, need, wait_one, 0)
        rows = pl.ds(pl.multiple_of(r * NEW, 8), NEW)
        table = pl.ds(pl.multiple_of(jnp.where(is_long, NEW, 0), 8), NEW)
        cos = cs_ref[table, pl.ds(0, HD)]
        sin = cs_ref[table, pl.ds(HD, HD)]
        rs = ss[rows, :]

        def rope(v):
            return v * cos + pltpu.roll(v, HD // 2, 1) * sin

        heads = []
        for g in range(GROUP):
            c = slice(g * HD, (g + 1) * HD)
            heads.append(rope(acc[rows, c] * rs + qb_ref[:, c]) * scale)
        heads.append(jnp.zeros((QR - GROUP * NEW, HD), jnp.float32))
        q = jnp.concatenate(heads, axis=0).astype(jnp.bfloat16)
        key = rope(acc[rows, QW : QW + HD] * rs + kvb_ref[:, 0:HD])
        value = acc[rows, QW + HD : QW + KW] * rs + kvb_ref[:, HD:KW]
        acc[rows, QW : QW + HD] = key
        acc[rows, QW + HD : QW + KW] = value
        fill = jnp.zeros((HD - NEW, HD), jnp.float32)
        key = jnp.concatenate([key, fill], axis=0).astype(jnp.bfloat16)
        value = jnp.concatenate([value, fill], axis=0).astype(jnp.bfloat16)

        def scores_of(k):
            return lax.dot_general(q, k, (((1,), (1,)), ((), ())), preferred_element_type=jnp.float32)

        def finish(n_chunks, width):
            s_new = jnp.where(causal, scores_of(key), NEG)
            chunks = []
            m = jnp.max(s_new, axis=1, keepdims=True)
            for i in range(n_chunks):
                w = pl.ds(pl.multiple_of(begin + i * width, SHORT), width)
                s = scores_of(pool_v[w, pl.ds(0, HD)])
                chunks.append((s, w))
                m = jnp.maximum(m, jnp.max(s, axis=1, keepdims=True))
            p = jnp.exp(s_new - m)
            total = jnp.sum(p, axis=1, keepdims=True)
            out = jnp.dot(p.astype(jnp.bfloat16), value, preferred_element_type=jnp.float32)
            for s, w in chunks:
                p = jnp.exp(s - m)
                total = total + jnp.sum(p, axis=1, keepdims=True)
                out = out + jnp.dot(
                    p.astype(jnp.bfloat16), pool_v[w, pl.ds(HD, HD)], preferred_element_type=jnp.float32
                )
            out = out / total
            for g in range(GROUP):
                acc[rows, g * HD : (g + 1) * HD] = out[g * NEW : (g + 1) * NEW, :]

        @pl.when(is_long)
        def _():
            finish(6, LONG // 6)

        @pl.when(jnp.logical_not(is_long))
        def _():
            finish(1, SHORT)

        return begin + length, jnp.maximum(waited, need)

    _, waited = lax.fori_loop(0, REQ_DEV, request, (jnp.int32(0), jnp.int32(0)))

    def wait_rest(i, c):
        pool_copy(i).wait()
        return c

    lax.fori_loop(waited, NPC, wait_rest, 0)
    attn_ref[...] = acc[:, 0:QW].astype(jnp.bfloat16)
    newkv_ref[...] = acc[:, QW : QW + KW].astype(jnp.bfloat16)
    last_ref[...] = jnp.concatenate(
        [acc[r * NEW + NEW - 1 : (r + 1) * NEW, 0:QW] for r in range(REQ_DEV)], axis=0
    ).astype(jnp.bfloat16)


def attention_call(cache_len, tokens, w_query, w_keyval, query_bias, keyval_bias, gain, pool):
    vmem = pl.BlockSpec(memory_space=pltpu.VMEM)
    hbm = pl.BlockSpec(memory_space=pl.ANY)
    smem = pl.BlockSpec(memory_space=pltpu.SMEM)
    return pl.pallas_call(
        attn_kernel,
        out_shape=(
            jax.ShapeDtypeStruct((ROWS, KW), jnp.bfloat16),
            jax.ShapeDtypeStruct((ROWS, QW), jnp.bfloat16),
            jax.ShapeDtypeStruct((REQ_DEV, QW), jnp.bfloat16),
        ),
        in_specs=[smem, hbm, hbm, hbm, vmem, vmem, vmem, vmem, hbm],
        out_specs=(vmem, vmem, vmem),
        scratch_shapes=[
            pltpu.VMEM((ROWS, D), jnp.bfloat16),
            pltpu.VMEM((D, QW + KW), jnp.bfloat16),
            pltpu.VMEM((POOL, KW), jnp.bfloat16),
            pltpu.VMEM((ROWS, QW + KW), jnp.float32),
            pltpu.VMEM((ROWS, HD), jnp.float32),
            pltpu.SemaphoreType.DMA((NKC,)),
            pltpu.SemaphoreType.DMA((NKC,)),
            pltpu.SemaphoreType.DMA((NKC,)),
            pltpu.SemaphoreType.DMA((NPC,)),
        ],
        compiler_params=pltpu.CompilerParams(vmem_limit_bytes=48 * 1024 * 1024),
        name="attend",
    )(
        cache_len,
        tokens,
        w_query,
        w_keyval,
        query_bias.reshape(1, QW),
        keyval_bias.reshape(1, KW),
        gain.reshape(1, D),
        jnp.asarray(rope_tables()),
        pool,
    )


def local(
    tokens,
    w_query,
    query_bias,
    w_keyval,
    keyval_bias,
    w_out,
    attn_gain,
    final_norm_gain,
    head_weight,
    kv_pool,
    cache_len,
):
    tp_count = lax.axis_size("tp")
    tp_index = lax.axis_index("tp")
    new_kv, attention, attn_last = attention_call(
        cache_len,
        tokens,
        w_query,
        w_keyval,
        query_bias,
        keyval_bias,
        attn_gain,
        kv_pool.reshape(POOL, KW),
    )
    new_kv = new_kv.reshape(ROWS, 1, KW)
    width_local = D // tp_count
    partial_value = jnp.dot(attention, w_out, preferred_element_type=jnp.float32)
    summed = lax.psum(partial_value.astype(jnp.bfloat16), "tp").astype(jnp.float32)
    states_full = (tokens.astype(jnp.float32) + summed).astype(jnp.bfloat16)
    states = lax.dynamic_slice_in_dim(states_full, tp_index * width_local, width_local, 1)
    last_rows = states_full.reshape(REQ_DEV, NEW, D)[:, NEW - 1, :].astype(jnp.float32)
    row_norms = jnp.sqrt(jnp.mean(last_rows * last_rows, axis=1) + EPS)
    final_rows = (last_rows / row_norms[:, None] * final_norm_gain[None, :]).astype(jnp.bfloat16)
    logits = jnp.dot(
        lax.all_gather(final_rows, "req", axis=0, tiled=True),
        head_weight,
        preferred_element_type=jnp.float32,
    )
    logit_max = lax.pmax(jnp.max(logits, axis=1), ("req", "tp"))
    return (states, new_kv, row_norms, logit_max, logits)


def solution(mesh):
    return jax.shard_map(
        local,
        mesh=mesh,
        in_specs=(
            P("req", None),
            P(None, "tp"),
            P("tp"),
            P(None, "tp"),
            P("tp"),
            P("tp", None),
            P(),
            P(),
            P(None, ("req", "tp")),
            P("req", "tp", None),
            P(),
        ),
        out_specs=(P("req", "tp"), P("req", "tp", None), P("req"), P(), P(None, ("req", "tp"))),
        check_vma=False,
    )
```

```python
import math

import jax
import jax.numpy as jnp
import numpy as np
from jax import lax
from jax.experimental import pallas as pl
from jax.experimental.pallas import tpu as pltpu
from jax.sharding import PartitionSpec as P

D = 5120
HD = 128
GROUP = 5
NEW = 24
SHORT = 256
LONG = 3072
REQ_DEV = 16
POOL = 26624
ROWS = REQ_DEV * NEW
QW = GROUP * HD
KW = 2 * HD
THETA = 1000000.0
EPS = 1e-06
NEG = -1e30

KC = 1024
NKC = D // KC
PC = 2048
NPC = POOL // PC
QR = 128


def rope_tables():
    freq = np.float32(THETA) ** (-(np.arange(HD // 2, dtype=np.float32) * np.float32(2.0 / HD)))
    pos = np.concatenate([SHORT + np.arange(NEW), LONG + np.arange(NEW)]).astype(np.float32)
    ang = (pos[:, None] * freq[None, :].astype(np.float32)).astype(np.float64)
    cos = np.cos(ang).astype(np.float32)
    sin = np.sin(ang).astype(np.float32)
    return np.concatenate([cos, cos, -sin, sin], axis=1)


def attn_kernel(
    lens_ref,
    tok_hbm,
    wq_hbm,
    wkv_hbm,
    qb_ref,
    kvb_ref,
    gain_ref,
    cs_ref,
    pool_hbm,
    newkv_ref,
    attn_ref,
    tok_v,
    w_v,
    pool_v,
    acc,
    ss,
    tok_sem,
    wq_sem,
    wkv_sem,
    pool_sem,
):
    def tok_copy(k):
        c = pl.ds(pl.multiple_of(k * KC, KC), KC)
        return pltpu.make_async_copy(tok_hbm.at[:, c], tok_v.at[:, c], tok_sem.at[k])

    def wq_copy(k):
        c = pl.ds(pl.multiple_of(k * KC, KC), KC)
        return pltpu.make_async_copy(wq_hbm.at[c, :], w_v.at[c, pl.ds(0, QW)], wq_sem.at[k])

    def wkv_copy(k):
        c = pl.ds(pl.multiple_of(k * KC, KC), KC)
        return pltpu.make_async_copy(wkv_hbm.at[c, :], w_v.at[c, pl.ds(QW, KW)], wkv_sem.at[k])

    def pool_copy(k):
        c = pl.ds(pl.multiple_of(k * PC, PC), PC)
        return pltpu.make_async_copy(pool_hbm.at[c, :], pool_v.at[c, :], pool_sem.at[k])

    for k in range(NKC):
        tok_copy(k).start()
        wq_copy(k).start()
        wkv_copy(k).start()
    for k in range(NPC):
        pool_copy(k).start()

    ss[...] = jnp.zeros_like(ss)
    acc[...] = jnp.zeros_like(acc)

    @pl.loop(0, NKC)
    def _(k):
        tok_copy(k).wait()
        wq_copy(k).wait()
        wkv_copy(k).wait()
        c = pl.ds(pl.multiple_of(k * KC, KC), KC)
        x = tok_v[:, c].astype(jnp.float32)
        sq = x * x
        part = sq[:, 0:HD]
        for i in range(1, KC // HD):
            part = part + sq[:, i * HD : (i + 1) * HD]
        ss[...] += part
        xg = (x * gain_ref[:, c]).astype(jnp.bfloat16)
        acc[...] += jnp.dot(xg, w_v[c, :], preferred_element_type=jnp.float32)

    rstd = 1.0 / jnp.sqrt(jnp.sum(ss[...], axis=1, keepdims=True) * (1.0 / D) + EPS)
    ss[...] = jnp.broadcast_to(rstd, ss.shape)

    row = lax.broadcasted_iota(jnp.int32, (QR, HD), 0)
    col = lax.broadcasted_iota(jnp.int32, (QR, HD), 1)
    token = row
    for g in range(1, GROUP + 1):
        token = token - jnp.where(row >= g * NEW, NEW, 0)
    causal = (col <= token) & (col < NEW)
    base = lax.axis_index("req") * REQ_DEV
    scale = 1.0 / math.sqrt(HD)

    def request(r, carry):
        begin, waited = carry
        length = lens_ref[base + r]
        is_long = length > SHORT
        need = (begin + length + (PC - 1)) // PC

        def wait_one(i, c):
            pool_copy(i).wait()
            return c

        lax.fori_loop(waited, need, wait_one, 0)
        rows = pl.ds(pl.multiple_of(r * NEW, 8), NEW)
        table = pl.ds(pl.multiple_of(jnp.where(is_long, NEW, 0), 8), NEW)
        cos = cs_ref[table, pl.ds(0, HD)]
        sin = cs_ref[table, pl.ds(HD, HD)]
        rs = ss[rows, :]

        def rope(v):
            return v * cos + pltpu.roll(v, HD // 2, 1) * sin

        heads = []
        for g in range(GROUP):
            c = slice(g * HD, (g + 1) * HD)
            heads.append(rope(acc[rows, c] * rs + qb_ref[:, c]) * scale)
        heads.append(jnp.zeros((QR - GROUP * NEW, HD), jnp.float32))
        q = jnp.concatenate(heads, axis=0).astype(jnp.bfloat16)
        key = rope(acc[rows, QW : QW + HD] * rs + kvb_ref[:, 0:HD])
        value = acc[rows, QW + HD : QW + KW] * rs + kvb_ref[:, HD:KW]
        acc[rows, QW : QW + HD] = key
        acc[rows, QW + HD : QW + KW] = value
        fill = jnp.zeros((HD - NEW, HD), jnp.float32)
        key = jnp.concatenate([key, fill], axis=0).astype(jnp.bfloat16)
        value = jnp.concatenate([value, fill], axis=0).astype(jnp.bfloat16)

        def scores_of(k):
            return lax.dot_general(q, k, (((1,), (1,)), ((), ())), preferred_element_type=jnp.float32)

        def finish(n_chunks, width):
            s_new = jnp.where(causal, scores_of(key), NEG)
            chunks = []
            m = jnp.max(s_new, axis=1, keepdims=True)
            for i in range(n_chunks):
                w = pl.ds(pl.multiple_of(begin + i * width, SHORT), width)
                s = scores_of(pool_v[w, pl.ds(0, HD)])
                chunks.append((s, w))
                m = jnp.maximum(m, jnp.max(s, axis=1, keepdims=True))
            p = jnp.exp(s_new - m)
            total = jnp.sum(p, axis=1, keepdims=True)
            out = jnp.dot(p.astype(jnp.bfloat16), value, preferred_element_type=jnp.float32)
            for s, w in chunks:
                p = jnp.exp(s - m)
                total = total + jnp.sum(p, axis=1, keepdims=True)
                out = out + jnp.dot(
                    p.astype(jnp.bfloat16), pool_v[w, pl.ds(HD, HD)], preferred_element_type=jnp.float32
                )
            out = out / total
            for g in range(GROUP):
                acc[rows, g * HD : (g + 1) * HD] = out[g * NEW : (g + 1) * NEW, :]

        @pl.when(is_long)
        def _():
            finish(6, LONG // 6)

        @pl.when(jnp.logical_not(is_long))
        def _():
            finish(1, SHORT)

        return begin + length, jnp.maximum(waited, need)

    _, waited = lax.fori_loop(0, REQ_DEV, request, (jnp.int32(0), jnp.int32(0)))

    def wait_rest(i, c):
        pool_copy(i).wait()
        return c

    lax.fori_loop(waited, NPC, wait_rest, 0)
    attn_ref[...] = acc[:, 0:QW].astype(jnp.bfloat16)
    newkv_ref[...] = acc[:, QW : QW + KW].astype(jnp.bfloat16)


def attention_call(cache_len, tokens, w_query, w_keyval, query_bias, keyval_bias, gain, pool):
    vmem = pl.BlockSpec(memory_space=pltpu.VMEM)
    hbm = pl.BlockSpec(memory_space=pl.ANY)
    smem = pl.BlockSpec(memory_space=pltpu.SMEM)
    return pl.pallas_call(
        attn_kernel,
        out_shape=(
            jax.ShapeDtypeStruct((ROWS, KW), jnp.bfloat16),
            jax.ShapeDtypeStruct((ROWS, QW), jnp.bfloat16),
        ),
        in_specs=[smem, hbm, hbm, hbm, vmem, vmem, vmem, vmem, hbm],
        out_specs=(vmem, vmem),
        scratch_shapes=[
            pltpu.VMEM((ROWS, D), jnp.bfloat16),
            pltpu.VMEM((D, QW + KW), jnp.bfloat16),
            pltpu.VMEM((POOL, KW), jnp.bfloat16),
            pltpu.VMEM((ROWS, QW + KW), jnp.float32),
            pltpu.VMEM((ROWS, HD), jnp.float32),
            pltpu.SemaphoreType.DMA((NKC,)),
            pltpu.SemaphoreType.DMA((NKC,)),
            pltpu.SemaphoreType.DMA((NKC,)),
            pltpu.SemaphoreType.DMA((NPC,)),
        ],
        compiler_params=pltpu.CompilerParams(vmem_limit_bytes=48 * 1024 * 1024),
        name="attend",
    )(
        cache_len,
        tokens,
        w_query,
        w_keyval,
        query_bias.reshape(1, QW),
        keyval_bias.reshape(1, KW),
        gain.reshape(1, D),
        jnp.asarray(rope_tables()),
        pool,
    )


CHUNKS = 4
CROWS = ROWS // CHUNKS
HROWS = CROWS // 2
TP = 4
WIDTH = D // TP
NT = 256
HALF = D // 2
QUART = HALF // 2
VLOC = 594
GROUP_ROWS = 128
MESH = pl.DeviceIdType.MESH
N_COPIES = 112


def tail_kernel(
    attn_ref,
    gain_ref,
    tok_hbm,
    wo_hbm,
    hw_hbm,
    states_ref,
    norms_ref,
    max_ref,
    logits_ref,
    tok_v,
    wo_v,
    hw_v,
    gathered,
    final,
    last_out,
    last_in,
    far_out,
    far_l,
    far_r,
    part_r,
    part_l,
    part_own,
    near_out_r,
    near_out_l,
    near_in_l,
    near_in_r,
    mx,
    mx_in,
    tok_sem,
    wo_sem,
    hw_sem,
    send_sem,
    recv_sem,
):
    req = lax.axis_index("req")
    y = lax.axis_index("tp")
    core = lax.rem(req, 2)
    x = lax.rem(req // 2, 4)
    z = req // 8
    right, left, opp = lax.rem(y + 1, TP), lax.rem(y + 3, TP), lax.rem(y + 2, TP)

    def at(dx=0, dz=0, dc=0, dy=0):
        xx, zz, cc = lax.rem(x + dx, 4), lax.rem(z + dz, 4), lax.rem(core + dc, 2)
        return {"req": (zz * 4 + xx) * 2 + cc, "tp": lax.rem(y + dy, TP)}

    peers = [at(dx=1), at(dx=2), at(dx=3), at(dz=1), at(dz=2), at(dz=3), at(dy=1), at(dy=2), at(dy=3), at(dc=1)]

    def wide(d):
        return pl.ds(pl.multiple_of(d * WIDTH, WIDTH), WIDTH)

    tok_copy = pltpu.make_async_copy(tok_hbm.at[:, wide(y)], tok_v, tok_sem)
    hw_copy = pltpu.make_async_copy(hw_hbm, hw_v, hw_sem)
    wo_copies = {}
    for i, d in enumerate((opp, right, left, y)):
        wo_copies[i] = pltpu.make_async_copy(wo_hbm.at[:, wide(d)], wo_v.at[i], wo_sem.at[i])
        wo_copies[i].start()
    tok_copy.start()
    hw_copy.start()

    barrier = pltpu.get_barrier_semaphore()
    for peer in peers:
        pl.semaphore_signal(barrier, inc=1, device_id=peer, device_id_type=MESH)
    pl.semaphore_wait(barrier, len(peers))

    copies = {}

    def send(name, src, dst, device):
        i = len(copies)
        copies[name] = pltpu.make_async_remote_copy(
            src_ref=src,
            dst_ref=dst,
            send_sem=send_sem.at[i],
            recv_sem=recv_sem.at[i],
            device_id=device,
            device_id_type=MESH,
        )
        copies[name].start()

    def got(name):
        copies[name].wait_recv()

    pick_row = lax.broadcasted_iota(jnp.int32, (REQ_DEV, ROWS), 0)
    pick_col = lax.broadcasted_iota(jnp.int32, (REQ_DEV, ROWS), 1)
    pick = (pick_col == pick_row * NEW + (NEW - 1)).astype(jnp.bfloat16)
    attn_last = jnp.dot(pick, attn_ref[...], preferred_element_type=jnp.float32).astype(jnp.bfloat16)

    for i, dy in enumerate((2, 1, 3)):
        wo_copies[i].wait()
        last_out[i] = jnp.dot(attn_last, wo_v[i], preferred_element_type=jnp.float32).astype(jnp.bfloat16)
        send(("last", dy), last_out.at[i], last_in.at[i], at(dy=dy))
    wo_copies[3].wait()

    def project(i, out_ref):
        @pl.loop(0, WIDTH // NT)
        def _(t):
            c = pl.ds(pl.multiple_of(t * NT, NT), NT)
            out_ref[:, c] = jnp.dot(
                attn_ref[...], wo_v[i, :, c], preferred_element_type=jnp.float32
            ).astype(out_ref.dtype)

    def far_send(c):
        r = c * CROWS
        send(("far", c, 1), far_out.at[r : r + HROWS], far_l.at[c], at(dy=1))
        send(("far", c, 3), far_out.at[r + HROWS : r + CROWS], far_r.at[c], at(dy=3))

    own_last = jnp.dot(attn_last, wo_v[3], preferred_element_type=jnp.float32)
    project(0, far_out)
    far_send(0)
    tok_copy.wait()
    own_last = own_last + jnp.dot(pick, tok_v[...], preferred_element_type=jnp.float32)
    for i, dy in enumerate((2, 1, 3)):
        got(("last", dy))
        own_last = own_last + last_in[i].astype(jnp.float32)
    own_rows = pl.ds(pl.multiple_of(req * REQ_DEV, REQ_DEV), REQ_DEV)
    gathered[own_rows, wide(y)] = own_last.astype(jnp.bfloat16)
    for dy in (1, 3, 2):
        block = gathered.at[own_rows, wide(y)]
        send(("slice", dy), block, block, at(dy=dy))
    far_send(1)
    project(1, part_r)
    project(2, part_l)
    for dy in (1, 3, 2):
        got(("slice", dy))

    def device(half, df=0, ds=0):
        return at(dx=df, dz=ds) if half == 0 else at(dx=ds, dz=df)

    def piece(half, df, ds, part=None):
        d = device(half, df, ds)["req"]
        rows = pl.ds(pl.multiple_of(d * REQ_DEV, REQ_DEV), REQ_DEV)
        start, width = half * HALF, HALF
        if part is not None:
            start, width = start + part * QUART, QUART
        return gathered.at[rows, start : start + width]

    def push(name, half, df, ds, to, part=None):
        block = piece(half, df, ds, part)
        send((name, half, df, ds, part), block, block, to)

    def spread(half, k):
        for side in (1, 3):
            block = piece(half, k, 0)
            send(("second", half, k, side), block, block, device(half, 0, side))

    def sibling(half, df, ds):
        push("sib", half, df, ds, at(dc=1))

    for half in (0, 1):
        for side in (1, 3):
            block = piece(half, 0, 0)
            send(("first", half, side), block, block, device(half, side, 0))
    for half in (0, 1):
        spread(half, 0)
    for half in (0, 1):
        sibling(half, 0, 0)

    own_state = gathered[own_rows, :].astype(jnp.float32)
    own_norm = jnp.sqrt(jnp.sum(own_state * own_state, axis=1, keepdims=True) * (1.0 / D) + EPS)
    eye_row = lax.broadcasted_iota(jnp.int32, (REQ_DEV, REQ_DEV), 0)
    eye_col = lax.broadcasted_iota(jnp.int32, (REQ_DEV, REQ_DEV), 1)
    norms_ref[...] = jnp.sum(jnp.where(eye_row == eye_col, own_norm, 0.0), axis=0, keepdims=True)

    def near_step(c):
        r = c * CROWS
        got(("far", c, 1))
        near_out_r[c, 0:HROWS] = (part_r[r : r + HROWS] + far_l[c].astype(jnp.float32)).astype(jnp.bfloat16)
        near_out_r[c, HROWS:CROWS] = part_r[r + HROWS : r + CROWS].astype(jnp.bfloat16)
        send(("near", c, 1), near_out_r.at[c], near_in_l.at[c], at(dy=1))
        got(("far", c, 3))
        near_out_l[c, 0:HROWS] = part_l[r : r + HROWS].astype(jnp.bfloat16)
        near_out_l[c, HROWS:CROWS] = (part_l[r + HROWS : r + CROWS] + far_r[c].astype(jnp.float32)).astype(jnp.bfloat16)
        send(("near", c, 3), near_out_l.at[c], near_in_r.at[c], at(dy=3))

    def relay_second(half, k):
        for side, part, ds in ((1, 0, 3), (3, 1, 1)):
            got(("second", half, k, side))
            block = piece(half, k, ds, part)
            send(("third", half, k, side), block, block, device(half, 0, side))
            sibling(half, k, ds)

    def finish_second(half, k):
        for side in (1, 3):
            got(("third", half, k, side))
        sibling(half, k, 2)

    def logits_of(dz):
        zz = lax.rem(z + dz, 4)
        for dx in range(4):
            got(("sib", 0, dx, dz, None))
            got(("sib", 1, dz, dx, None))

        @pl.loop(0, GROUP_ROWS // REQ_DEV)
        def _(t):
            src = pl.ds(pl.multiple_of(zz * GROUP_ROWS + t * REQ_DEV, REQ_DEV), REQ_DEV)
            g = gathered[src, :].astype(jnp.float32)
            inv = 1.0 / jnp.sqrt(jnp.sum(g * g, axis=1, keepdims=True) * (1.0 / D) + EPS)
            dst = pl.ds(pl.multiple_of(t * REQ_DEV, REQ_DEV), REQ_DEV)
            final[dst, :] = (g * inv * gain_ref[...]).astype(jnp.bfloat16)

        out = lax.dot_general(
            hw_v[...], final[...], (((1,), (1,)), ((), ())), preferred_element_type=jnp.float32
        )
        logits_ref[:, pl.ds(pl.multiple_of(zz * GROUP_ROWS, GROUP_ROWS), GROUP_ROWS)] = out
        mx[0, pl.ds(zz, 1), :] = jnp.max(out, axis=0, keepdims=True)

    far_send(2)
    far_send(3)
    for half in (0, 1):
        for side, part, df in ((1, 0, 3), (3, 1, 1)):
            got(("first", half, side))
            block = piece(half, df, 0, part)
            send(("relay", half, side), block, block, device(half, side, 0))
            spread(half, df)
            sibling(half, df, 0)
    near_step(0)
    for half in (0, 1):
        relay_second(half, 0)
    for half in (0, 1):
        for side in (1, 3):
            got(("relay", half, side))
        spread(half, 2)
        sibling(half, 2, 0)
    near_step(1)
    project(3, part_own)
    for k in (3, 1):
        for half in (0, 1):
            relay_second(half, k)
    near_step(2)
    for half in (0, 1):
        finish_second(half, 0)
    near_step(3)
    hw_copy.wait()
    logits_of(0)
    for half in (0, 1):
        relay_second(half, 2)
    for k in (3, 1):
        for half in (0, 1):
            finish_second(half, k)
    logits_of(1)
    logits_of(3)
    for half in (0, 1):
        finish_second(half, 2)
    logits_of(2)

    def spread_max(stage, moves):
        for i, move in enumerate(moves):
            send(("max", stage, i), mx.at[stage], mx_in.at[stage, i], at(**move))

    def take_max(stage, moves):
        m = mx[stage]
        for i in range(len(moves)):
            got(("max", stage, i))
            m = jnp.maximum(m, mx_in[stage, i])
        return m

    stages = [
        [{"dc": 1}],
        [{"dx": 1}, {"dx": 3}, {"dx": 2}],
        [{"dz": 1}, {"dz": 3}, {"dz": 2}],
        [{"dy": 1}, {"dy": 3}, {"dy": 2}],
    ]
    for s in range(3):
        spread_max(s, stages[s])
        mx[s + 1] = take_max(s, stages[s])
    spread_max(3, stages[3])

    for c in range(CHUNKS):
        r = slice(c * CROWS, (c + 1) * CROWS)
        got(("near", c, 1))
        got(("near", c, 3))
        total = tok_v[r].astype(jnp.float32) + part_own[r] + near_in_l[c].astype(jnp.float32)
        states_ref[r] = (total + near_in_r[c].astype(jnp.float32)).astype(jnp.bfloat16)
    max_ref[...] = take_max(3, stages[3])
    for c in copies.values():
        c.wait_send()


def tail_call(attention, gain, tokens, w_out, head_t):
    vmem = pl.BlockSpec(memory_space=pltpu.VMEM)
    hbm = pl.BlockSpec(memory_space=pl.ANY)
    half = jnp.bfloat16
    return pl.pallas_call(
        tail_kernel,
        out_shape=(
            jax.ShapeDtypeStruct((ROWS, WIDTH), half),
            jax.ShapeDtypeStruct((1, REQ_DEV), jnp.float32),
            jax.ShapeDtypeStruct((4, GROUP_ROWS), jnp.float32),
            jax.ShapeDtypeStruct((VLOC, 4 * GROUP_ROWS), jnp.float32),
        ),
        in_specs=[vmem, vmem, hbm, hbm, hbm],
        out_specs=(vmem, vmem, vmem, vmem),
        scratch_shapes=[
            pltpu.VMEM((ROWS, WIDTH), half),
            pltpu.VMEM((TP, QW, WIDTH), half),
            pltpu.VMEM((VLOC, D), half),
            pltpu.VMEM((4 * GROUP_ROWS, D), half),
            pltpu.VMEM((GROUP_ROWS, D), half),
            pltpu.VMEM((3, REQ_DEV, WIDTH), half),
            pltpu.VMEM((3, REQ_DEV, WIDTH), half),
            pltpu.VMEM((ROWS, WIDTH), half),
            pltpu.VMEM((CHUNKS, HROWS, WIDTH), half),
            pltpu.VMEM((CHUNKS, HROWS, WIDTH), half),
            pltpu.VMEM((ROWS, WIDTH), jnp.float32),
            pltpu.VMEM((ROWS, WIDTH), jnp.float32),
            pltpu.VMEM((ROWS, WIDTH), jnp.float32),
            pltpu.VMEM((CHUNKS, CROWS, WIDTH), half),
            pltpu.VMEM((CHUNKS, CROWS, WIDTH), half),
            pltpu.VMEM((CHUNKS, CROWS, WIDTH), half),
            pltpu.VMEM((CHUNKS, CROWS, WIDTH), half),
            pltpu.VMEM((4, 4, GROUP_ROWS), jnp.float32),
            pltpu.VMEM((4, 3, 4, GROUP_ROWS), jnp.float32),
            pltpu.SemaphoreType.DMA,
            pltpu.SemaphoreType.DMA((TP,)),
            pltpu.SemaphoreType.DMA,
            pltpu.SemaphoreType.DMA((N_COPIES,)),
            pltpu.SemaphoreType.DMA((N_COPIES,)),
        ],
        compiler_params=pltpu.CompilerParams(
            vmem_limit_bytes=52 * 1024 * 1024, collective_id=0, has_side_effects=True
        ),
        name="tail",
    )(attention, gain.reshape(1, D), tokens, w_out, head_t)


def local(
    tokens,
    w_query,
    query_bias,
    w_keyval,
    keyval_bias,
    w_out,
    attn_gain,
    final_norm_gain,
    head_weight,
    kv_pool,
    cache_len,
):
    new_kv, attention = attention_call(
        cache_len,
        tokens,
        w_query,
        w_keyval,
        query_bias,
        keyval_bias,
        attn_gain,
        kv_pool.reshape(POOL, KW),
    )
    states, norms, top, logits_t = tail_call(attention, final_norm_gain, tokens, w_out, head_weight.T)
    return (
        states,
        new_kv.reshape(ROWS, 1, KW),
        norms.reshape(REQ_DEV),
        top.reshape(4 * GROUP_ROWS),
        logits_t.T,
    )


def solution(mesh):
    return jax.shard_map(
        local,
        mesh=mesh,
        in_specs=(
            P("req", None),
            P(None, "tp"),
            P("tp"),
            P(None, "tp"),
            P("tp"),
            P("tp", None),
            P(),
            P(),
            P(None, ("req", "tp")),
            P("req", "tp", None),
            P(),
        ),
        out_specs=(P("req", "tp"), P("req", "tp", None), P("req"), P(), P(None, ("req", "tp"))),
        check_vma=False,
    )
```

```python
import math

import jax
import jax.numpy as jnp
import numpy as np
from jax import lax
from jax.experimental import pallas as pl
from jax.experimental.pallas import tpu as pltpu
from jax.sharding import PartitionSpec as P

D = 5120
HD = 128
GROUP = 5
NEW = 24
SHORT = 256
LONG = 3072
REQ_DEV = 16
REQUESTS = 512
POOL = 26624
ROWS = REQ_DEV * NEW
QW = GROUP * HD
KW = 2 * HD
THETA = 1000000.0
EPS = 1e-06
NEG = -1e30

KC = 1024
NKC = D // KC
PC = 2048
NPC = POOL // PC
QR = 128
PER_STEP = 4
BATCH = 4
WIDE = (LONG - SHORT) // 2
VLOC = 594


def rope_tables():
    freq = np.float32(THETA) ** (-(np.arange(HD // 2, dtype=np.float32) * np.float32(2.0 / HD)))
    pos = np.concatenate([SHORT + np.arange(NEW), LONG + np.arange(NEW)]).astype(np.float32)
    ang = (pos[:, None] * freq[None, :].astype(np.float32)).astype(np.float64)
    cos = np.cos(ang).astype(np.float32)
    sin = np.sin(ang).astype(np.float32)
    return np.concatenate([cos, cos, -sin, sin], axis=1)


def attn_kernel(
    lens_hbm,
    tok_hbm,
    wq_hbm,
    wkv_hbm,
    qb_hbm,
    kvb_hbm,
    gain_hbm,
    cs_hbm,
    pool_hbm,
    wo_hbm,
    hw_hbm,
    newkv_ref,
    attn_ref,
    wo_ref,
    hw_ref,
    tok_v,
    w_v,
    pool_v,
    acc,
    ss,
    att_s,
    kv_s,
    q_s,
    m_s,
    l_s,
    o_s,
    lens_ref,
    start_ref,
    long_ref,
    qb_v,
    kvb_v,
    gain_v,
    cs_ref,
    tok_sem,
    wq_sem,
    wkv_sem,
    pool_sem,
    small_sem,
    tail_sem,
):
    def tok_copy(k):
        c = pl.ds(pl.multiple_of(k * KC, KC), KC)
        return pltpu.make_async_copy(tok_hbm.at[:, c], tok_v.at[:, c], tok_sem.at[k])

    def wq_copy(k):
        c = pl.ds(pl.multiple_of(k * KC, KC), KC)
        return pltpu.make_async_copy(wq_hbm.at[c, :], w_v.at[c, pl.ds(0, QW)], wq_sem.at[k])

    def wkv_copy(k):
        c = pl.ds(pl.multiple_of(k * KC, KC), KC)
        return pltpu.make_async_copy(wkv_hbm.at[c, :], w_v.at[c, pl.ds(QW, KW)], wkv_sem.at[k])

    def pool_copy(k):
        c = pl.ds(pl.multiple_of(k * PC, PC), PC)
        return pltpu.make_async_copy(pool_hbm.at[c, :], pool_v.at[c, :], pool_sem.at[k])

    smalls = [
        pltpu.make_async_copy(src, dst, small_sem.at[i])
        for i, (src, dst) in enumerate(
            ((gain_hbm, gain_v), (lens_hbm, lens_ref), (qb_hbm, qb_v), (kvb_hbm, kvb_v), (cs_hbm, cs_ref))
        )
    ]
    tails = [
        pltpu.make_async_copy(wo_hbm, wo_ref, tail_sem.at[0]),
        pltpu.make_async_copy(hw_hbm, hw_ref, tail_sem.at[1]),
    ]
    smalls[0].start()
    smalls[1].start()
    for k in range(NKC):
        tok_copy(k).start()
        wq_copy(k).start()
        wkv_copy(k).start()
    for c in smalls[2:]:
        c.start()
    ss[...] = jnp.zeros_like(ss)
    acc[...] = jnp.zeros_like(acc)
    base = lax.axis_index("req") * REQ_DEV
    smalls[1].wait()

    def place(r, carry):
        begin, n_long = carry
        length = lens_ref[base + r]
        start_ref[r] = begin
        long_ref[n_long] = r
        return begin + length, n_long + jnp.where(length > SHORT, 1, 0)

    _, n_long = lax.fori_loop(0, REQ_DEV, place, (jnp.int32(0), jnp.int32(0)))
    smalls[0].wait()

    for k in range(NKC):
        tok_copy(k).wait()
        wq_copy(k).wait()
        wkv_copy(k).wait()
        if k >= 1:
            for i in range(PER_STEP * (k - 1), min(PER_STEP * k, NPC)):
                pool_copy(i).start()
        c = slice(k * KC, (k + 1) * KC)
        x = tok_v[:, c].astype(jnp.float32)
        sq = x * x
        part = sq[:, 0:HD]
        for i in range(1, KC // HD):
            part = part + sq[:, i * HD : (i + 1) * HD]
        ss[...] += part
        xg = (x * gain_v[c].reshape(1, KC)).astype(jnp.bfloat16)
        acc[...] += jnp.dot(xg, w_v[c, :], preferred_element_type=jnp.float32)
    for c in tails:
        c.start()

    for c in smalls[2:]:
        c.wait()
    rstd = 1.0 / jnp.sqrt(jnp.sum(ss[...], axis=1, keepdims=True) * (1.0 / D) + EPS)
    ss[...] = jnp.broadcast_to(rstd, ss.shape)

    row = lax.broadcasted_iota(jnp.int32, (QR, HD), 0)
    col = lax.broadcasted_iota(jnp.int32, (QR, HD), 1)
    token = row
    for g in range(1, GROUP + 1):
        token = token - jnp.where(row >= g * NEW, NEW, 0)
    causal = (col <= token) & (col < NEW)
    scale = 1.0 / math.sqrt(HD)

    def wait_one(i, c):
        pool_copy(i).wait()
        return c

    def scores_of(q, k):
        return lax.dot_general(q, k, (((1,), (1,)), ((), ())), preferred_element_type=jnp.float32)

    def mix(p, v):
        return jnp.dot(p.astype(jnp.bfloat16), v, preferred_element_type=jnp.float32)

    def rows_of(r):
        return pl.ds(pl.multiple_of(r * NEW, 8), NEW)

    def store_heads(r, out):
        for g in range(GROUP):
            att_s[rows_of(r), g * HD : (g + 1) * HD] = out[g * NEW : (g + 1) * NEW, :]

    def batch(b, waited):
        ids = [b * BATCH + i for i in range(BATCH)]
        begins = [start_ref[r] for r in ids]
        need = (begins[-1] + SHORT + (PC - 1)) // PC
        lax.fori_loop(waited, need, wait_one, 0)
        fill = jnp.zeros((HD - NEW, HD), jnp.float32)
        qs, keys, values = [], [], []
        for r in ids:
            rows = rows_of(r)
            table = pl.ds(pl.multiple_of(jnp.where(lens_ref[base + r] > SHORT, NEW, 0), 8), NEW)
            cos = cs_ref[table, pl.ds(0, HD)]
            sin = cs_ref[table, pl.ds(HD, HD)]
            rs = ss[rows, :]

            def rope(v, cos=cos, sin=sin):
                return v * cos + pltpu.roll(v, HD // 2, 1) * sin

            heads = []
            for g in range(GROUP):
                c = slice(g * HD, (g + 1) * HD)
                heads.append(rope(acc[rows, c] * rs + qb_v[c].reshape(1, HD)) * scale)
            heads.append(jnp.zeros((QR - GROUP * NEW, HD), jnp.float32))
            qs.append(jnp.concatenate(heads, axis=0).astype(jnp.bfloat16))
            key = rope(acc[rows, QW : QW + HD] * rs + kvb_v[0:HD].reshape(1, HD))
            value = acc[rows, QW + HD : QW + KW] * rs + kvb_v[HD:KW].reshape(1, HD)
            kv_s[rows, 0:HD] = key
            kv_s[rows, HD:KW] = value
            keys.append(jnp.concatenate([key, fill], axis=0).astype(jnp.bfloat16))
            values.append(jnp.concatenate([value, fill], axis=0).astype(jnp.bfloat16))
        windows = [pl.ds(pl.multiple_of(x, SHORT), SHORT) for x in begins]
        old = [scores_of(q, pool_v[w, pl.ds(0, HD)]) for q, w in zip(qs, windows)]
        new = [jnp.where(causal, scores_of(q, k), NEG) for q, k in zip(qs, keys)]
        ms = [
            jnp.maximum(jnp.max(s, axis=1, keepdims=True), jnp.max(t, axis=1, keepdims=True))
            for s, t in zip(old, new)
        ]
        p_old = [jnp.exp(s - m) for s, m in zip(old, ms)]
        p_new = [jnp.exp(t - m) for t, m in zip(new, ms)]
        ls = [
            jnp.sum(p, axis=1, keepdims=True) + jnp.sum(u, axis=1, keepdims=True)
            for p, u in zip(p_old, p_new)
        ]
        outs = [
            mix(p, pool_v[w, pl.ds(HD, HD)]) + mix(u, v)
            for p, u, w, v in zip(p_old, p_new, windows, values)
        ]
        for i, r in enumerate(ids):
            q_s[r] = qs[i]
            m_s[r] = jnp.broadcast_to(ms[i], (QR, HD))
            l_s[r] = jnp.broadcast_to(ls[i], (QR, HD))
            o_s[r] = outs[i]
            store_heads(r, outs[i] / ls[i])
        return jnp.maximum(waited, need)

    waited = lax.fori_loop(0, REQ_DEV // BATCH, batch, jnp.int32(0))
    lax.fori_loop(waited, NPC, wait_one, 0)

    def longs(j, carry):
        ids = [long_ref[2 * j], long_ref[jnp.minimum(2 * j + 1, n_long - 1)]]
        begins = [pl.multiple_of(start_ref[r] + SHORT, SHORT) for r in ids]
        qs = [q_s[r] for r in ids]
        windows = [
            [pl.ds(pl.multiple_of(x + i * WIDE, HD), WIDE) for i in range((LONG - SHORT) // WIDE)] for x in begins
        ]
        scores = [[scores_of(q, pool_v[w, pl.ds(0, HD)]) for w in ws] for q, ws in zip(qs, windows)]
        outs = []
        for r, ws, parts in zip(ids, windows, scores):
            before = m_s[r][:, 0:1]
            m = before
            for s in parts:
                m = jnp.maximum(m, jnp.max(s, axis=1, keepdims=True))
            fade = jnp.exp(before - m)
            total = l_s[r][:, 0:1] * fade
            out = o_s[r] * fade
            for s, w in zip(parts, ws):
                p = jnp.exp(s - m)
                total = total + jnp.sum(p, axis=1, keepdims=True)
                out = out + mix(p, pool_v[w, pl.ds(HD, HD)])
            outs.append(out / total)
        for r, out in zip(ids, outs):
            store_heads(r, out)
        return carry

    lax.fori_loop(0, (n_long + 1) // 2, longs, 0)
    attn_ref[...] = att_s[...].astype(jnp.bfloat16)
    newkv_ref[...] = kv_s[...].astype(jnp.bfloat16)
    for c in tails:
        c.wait()


def in_hbm(a):
    return pltpu.with_memory_space_constraint(a, pltpu.HBM)


def attention_call(cache_len, tokens, w_query, w_keyval, query_bias, keyval_bias, gain, pool, w_out, head_t):
    vmem = pl.BlockSpec(memory_space=pltpu.VMEM)
    hbm = pl.BlockSpec(memory_space=pltpu.HBM)
    return pl.pallas_call(
        attn_kernel,
        out_shape=(
            jax.ShapeDtypeStruct((ROWS, KW), jnp.bfloat16),
            jax.ShapeDtypeStruct((ROWS, QW), jnp.bfloat16),
            jax.ShapeDtypeStruct((QW, D), jnp.bfloat16),
            jax.ShapeDtypeStruct((VLOC, D), jnp.bfloat16),
        ),
        in_specs=[hbm] * 11,
        out_specs=(vmem, vmem, vmem, vmem),
        scratch_shapes=[
            pltpu.VMEM((ROWS, D), jnp.bfloat16),
            pltpu.VMEM((D, QW + KW), jnp.bfloat16),
            pltpu.VMEM((POOL, KW), jnp.bfloat16),
            pltpu.VMEM((ROWS, QW + KW), jnp.float32),
            pltpu.VMEM((ROWS, HD), jnp.float32),
            pltpu.VMEM((ROWS, QW), jnp.float32),
            pltpu.VMEM((ROWS, KW), jnp.float32),
            pltpu.VMEM((REQ_DEV, QR, HD), jnp.bfloat16),
            pltpu.VMEM((REQ_DEV, QR, HD), jnp.float32),
            pltpu.VMEM((REQ_DEV, QR, HD), jnp.float32),
            pltpu.VMEM((REQ_DEV, QR, HD), jnp.float32),
            pltpu.SMEM((REQUESTS,), jnp.int32),
            pltpu.SMEM((REQ_DEV,), jnp.int32),
            pltpu.SMEM((REQ_DEV + 1,), jnp.int32),
            pltpu.VMEM((QW,), jnp.float32),
            pltpu.VMEM((KW,), jnp.float32),
            pltpu.VMEM((D,), jnp.float32),
            pltpu.VMEM((2 * NEW, 2 * HD), jnp.float32),
            pltpu.SemaphoreType.DMA((NKC,)),
            pltpu.SemaphoreType.DMA((NKC,)),
            pltpu.SemaphoreType.DMA((NKC,)),
            pltpu.SemaphoreType.DMA((NPC,)),
            pltpu.SemaphoreType.DMA((5,)),
            pltpu.SemaphoreType.DMA((2,)),
        ],
        compiler_params=pltpu.CompilerParams(vmem_limit_bytes=36 * 1024 * 1024),
        name="attend",
    )(
        in_hbm(cache_len),
        in_hbm(tokens),
        in_hbm(w_query),
        in_hbm(w_keyval),
        in_hbm(query_bias),
        in_hbm(keyval_bias),
        in_hbm(gain),
        in_hbm(jnp.asarray(rope_tables())),
        in_hbm(pool),
        in_hbm(w_out),
        in_hbm(head_t),
    )


CHUNKS = 4
CROWS = ROWS // CHUNKS
HROWS = CROWS // 2
TP = 4
WIDTH = D // TP
HALF = D // 2
QUART = HALF // 2
PAIR = 256
MESH = pl.DeviceIdType.MESH
N_COPIES = 124


def tail_kernel(
    attn_ref,
    gain_ref,
    tok_hbm,
    wo_ref,
    hw_ref,
    states_ref,
    norms_ref,
    max_ref,
    logits_ref,
    tok_v,
    own_state,
    gathered,
    last_out,
    last_in,
    far_out,
    far_l,
    far_r,
    part_r,
    part_l,
    part_own,
    near_out_r,
    near_out_l,
    near_in_l,
    near_in_r,
    mx,
    mx_in,
    tok_sem,
    send_sem,
    recv_sem,
):
    req = lax.axis_index("req")
    y = lax.axis_index("tp")
    core = lax.rem(req, 2)
    x = lax.rem(req // 2, 4)
    z = req // 8
    right, left, opp = lax.rem(y + 1, TP), lax.rem(y + 3, TP), lax.rem(y + 2, TP)

    def at(dx=0, dz=0, dc=0, dy=0):
        xx, zz, cc = lax.rem(x + dx, 4), lax.rem(z + dz, 4), lax.rem(core + dc, 2)
        return {"req": (zz * 4 + xx) * 2 + cc, "tp": lax.rem(y + dy, TP)}

    plane = [{"dx": i, "dz": j} for i in range(4) for j in range(4) if i or j]
    column = [{"dy": i, "dc": j} for i in range(4) for j in range(2) if i or j]
    peers = [at(**move) for move in plane + column]

    def wide(d):
        return pl.ds(pl.multiple_of(d * WIDTH, WIDTH), WIDTH)

    tok_copy = pltpu.make_async_copy(tok_hbm.at[:, wide(y)], tok_v, tok_sem)
    tok_copy.start()

    barrier = pltpu.get_barrier_semaphore()
    for peer in peers:
        pl.semaphore_signal(barrier, inc=1, device_id=peer, device_id_type=MESH)

    copies = {}

    def send(name, src, dst, device):
        i = len(copies)
        copies[name] = pltpu.make_async_remote_copy(
            src_ref=src,
            dst_ref=dst,
            send_sem=send_sem.at[i],
            recv_sem=recv_sem.at[i],
            device_id=device,
            device_id_type=MESH,
        )
        copies[name].start()

    def got(name):
        copies[name].wait_recv()

    pick_row = lax.broadcasted_iota(jnp.int32, (REQ_DEV, ROWS), 0)
    pick_col = lax.broadcasted_iota(jnp.int32, (REQ_DEV, ROWS), 1)
    pick = (pick_col == pick_row * NEW + (NEW - 1)).astype(jnp.bfloat16)
    attn_last = jnp.dot(pick, attn_ref[...], preferred_element_type=jnp.float32).astype(jnp.bfloat16)

    def project(dy, out_ref):
        out_ref[...] = jnp.dot(
            attn_ref[...], wo_ref[:, wide(lax.rem(y + dy, TP))], preferred_element_type=jnp.float32
        ).astype(out_ref.dtype)

    def far_send(c):
        r = c * CROWS
        send(("far", c, 1), far_out.at[r : r + HROWS], far_l.at[c], at(dy=1))
        send(("far", c, 3), far_out.at[r + HROWS : r + CROWS], far_r.at[c], at(dy=3))

    order = ((2, 0), (1, 1), (3, 2))
    for dy, i in order:
        last_out[i] = jnp.dot(
            attn_last, wo_ref[:, wide(lax.rem(y + dy, TP))], preferred_element_type=jnp.float32
        ).astype(jnp.bfloat16)
    project(2, far_out)
    pl.semaphore_wait(barrier, len(peers))
    for dy, i in order:
        send(("last", dy), last_out.at[i], last_in.at[i], at(dy=dy))
    far_send(0)
    own_last = jnp.dot(attn_last, wo_ref[:, wide(y)], preferred_element_type=jnp.float32)
    tok_copy.wait()
    own_last = own_last + jnp.dot(pick, tok_v[...], preferred_element_type=jnp.float32)
    project(1, part_r)
    for dy, i in order:
        got(("last", dy))
        own_last = own_last + last_in[i].astype(jnp.float32)
    own_rows = pl.ds(pl.multiple_of(req * REQ_DEV, REQ_DEV), REQ_DEV)
    own_state[:, wide(y)] = own_last.astype(jnp.bfloat16)
    for dy in (1, 3, 2):
        block = own_state.at[:, wide(y)]
        send(("slice", dy), block, block, at(dy=dy))
    for c in range(1, CHUNKS):
        far_send(c)
    project(3, part_l)
    for dy in (1, 3, 2):
        got(("slice", dy))
    own = own_state[...].astype(jnp.float32)
    own_norm = jnp.sqrt(jnp.sum(own * own, axis=1, keepdims=True) * (1.0 / D) + EPS)
    gathered[own_rows, :] = (own / own_norm * gain_ref[...]).astype(jnp.bfloat16)

    def device(half, df=0, ds=0):
        return at(dx=df, dz=ds) if half == 0 else at(dx=ds, dz=df)

    def piece(half, df, ds, part=None):
        d = device(half, df, ds)["req"]
        rows = pl.ds(pl.multiple_of(d * REQ_DEV, REQ_DEV), REQ_DEV)
        start, width = half * HALF, HALF
        if part is not None:
            start, width = start + part * QUART, QUART
        return gathered.at[rows, start : start + width]

    def push(name, half, df, ds, to, part=None):
        block = piece(half, df, ds, part)
        send((name, half, df, ds, part), block, block, to)

    def spread(half, k):
        for side in (1, 3):
            block = piece(half, k, 0)
            send(("second", half, k, side), block, block, device(half, 0, side))

    def sibling(half, df, ds):
        push("sib", half, df, ds, at(dc=1))

    for half in (0, 1):
        for side in (1, 3):
            block = piece(half, 0, 0)
            send(("first", half, side), block, block, device(half, side, 0))
    for half in (0, 1):
        spread(half, 0)
    for half in (0, 1):
        sibling(half, 0, 0)

    eye_row = lax.broadcasted_iota(jnp.int32, (REQ_DEV, REQ_DEV), 0)
    eye_col = lax.broadcasted_iota(jnp.int32, (REQ_DEV, REQ_DEV), 1)
    norms_ref[...] = jnp.sum(jnp.where(eye_row == eye_col, own_norm, 0.0), axis=0, keepdims=True)

    def near_step(c):
        r = c * CROWS
        got(("far", c, 1))
        near_out_r[c, 0:HROWS] = (part_r[r : r + HROWS] + far_l[c].astype(jnp.float32)).astype(jnp.bfloat16)
        near_out_r[c, HROWS:CROWS] = part_r[r + HROWS : r + CROWS].astype(jnp.bfloat16)
        send(("near", c, 1), near_out_r.at[c], near_in_l.at[c], at(dy=1))
        got(("far", c, 3))
        near_out_l[c, 0:HROWS] = part_l[r : r + HROWS].astype(jnp.bfloat16)
        near_out_l[c, HROWS:CROWS] = (part_l[r + HROWS : r + CROWS] + far_r[c].astype(jnp.float32)).astype(jnp.bfloat16)
        send(("near", c, 3), near_out_l.at[c], near_in_r.at[c], at(dy=3))

    def relay_second(half, k):
        for side, part, ds in ((1, 0, 3), (3, 1, 1)):
            got(("second", half, k, side))
            block = piece(half, k, ds, part)
            send(("third", half, k, side), block, block, device(half, 0, side))
            sibling(half, k, ds)

    def finish_second(half, k):
        for side in (1, 3):
            got(("third", half, k, side))
        sibling(half, k, 2)

    def logits_of(pair, shifts):
        for dz in shifts:
            for dx in range(4):
                got(("sib", 0, dx, dz, None))
                got(("sib", 1, dz, dx, None))
        rows = pl.ds(pl.multiple_of(pair * PAIR, PAIR), PAIR)
        out = lax.dot_general(
            hw_ref[...], gathered[rows, :], (((1,), (1,)), ((), ())), preferred_element_type=jnp.float32
        )
        logits_ref[:, rows] = out
        mx[0, pl.ds(pair, 1), :] = jnp.max(out, axis=0, keepdims=True)

    project(0, part_own)
    for half in (0, 1):
        for side, part, df in ((1, 0, 3), (3, 1, 1)):
            got(("first", half, side))
            block = piece(half, df, 0, part)
            send(("relay", half, side), block, block, device(half, side, 0))
            spread(half, df)
            sibling(half, df, 0)
    near_step(0)
    for half in (0, 1):
        relay_second(half, 0)
    for half in (0, 1):
        for side in (1, 3):
            got(("relay", half, side))
        spread(half, 2)
        sibling(half, 2, 0)
    near_step(1)
    for k in (3, 1):
        for half in (0, 1):
            relay_second(half, k)
    near_step(2)
    for half in (0, 1):
        finish_second(half, 0)
    for half in (0, 1):
        relay_second(half, 2)
    near_step(3)
    for k in (3, 1):
        for half in (0, 1):
            finish_second(half, k)
    mine, other = z // 2, 1 - z // 2

    for half in (0, 1):
        finish_second(half, 2)
    logits_of(mine, (0, 1, 3))
    logits_of(other, (2,))

    def spread_max(stage, moves):
        for i, move in enumerate(moves):
            send(("max", stage, i), mx.at[stage], mx_in.at[stage, i], at(**move))

    def take_max(stage, moves):
        m = mx[stage]
        for i in range(len(moves)):
            got(("max", stage, i))
            m = jnp.maximum(m, mx_in[stage, i])
        return m

    spread_max(0, plane)
    mx[1] = take_max(0, plane)
    spread_max(1, column)

    for c in range(CHUNKS):
        r = slice(c * CROWS, (c + 1) * CROWS)
        got(("near", c, 1))
        got(("near", c, 3))
        total = tok_v[r].astype(jnp.float32) + part_own[r] + near_in_l[c].astype(jnp.float32)
        states_ref[r] = (total + near_in_r[c].astype(jnp.float32)).astype(jnp.bfloat16)
    max_ref[...] = take_max(1, column)
    for c in copies.values():
        c.wait_send()


def tail_call(attention, gain, tokens, w_out, head_t):
    vmem = pl.BlockSpec(memory_space=pltpu.VMEM)
    hbm = pl.BlockSpec(memory_space=pltpu.HBM)
    half = jnp.bfloat16
    return pl.pallas_call(
        tail_kernel,
        out_shape=(
            jax.ShapeDtypeStruct((ROWS, WIDTH), half),
            jax.ShapeDtypeStruct((1, REQ_DEV), jnp.float32),
            jax.ShapeDtypeStruct((2, PAIR), jnp.float32),
            jax.ShapeDtypeStruct((VLOC, 2 * PAIR), jnp.float32),
        ),
        in_specs=[vmem, vmem, hbm, vmem, vmem],
        out_specs=(vmem, vmem, vmem, vmem),
        scratch_shapes=[
            pltpu.VMEM((ROWS, WIDTH), half),
            pltpu.VMEM((REQ_DEV, D), half),
            pltpu.VMEM((2 * PAIR, D), half),
            pltpu.VMEM((3, REQ_DEV, WIDTH), half),
            pltpu.VMEM((3, REQ_DEV, WIDTH), half),
            pltpu.VMEM((ROWS, WIDTH), half),
            pltpu.VMEM((CHUNKS, HROWS, WIDTH), half),
            pltpu.VMEM((CHUNKS, HROWS, WIDTH), half),
            pltpu.VMEM((ROWS, WIDTH), jnp.float32),
            pltpu.VMEM((ROWS, WIDTH), jnp.float32),
            pltpu.VMEM((ROWS, WIDTH), jnp.float32),
            pltpu.VMEM((CHUNKS, CROWS, WIDTH), half),
            pltpu.VMEM((CHUNKS, CROWS, WIDTH), half),
            pltpu.VMEM((CHUNKS, CROWS, WIDTH), half),
            pltpu.VMEM((CHUNKS, CROWS, WIDTH), half),
            pltpu.VMEM((2, 2, PAIR), jnp.float32),
            pltpu.VMEM((2, 15, 2, PAIR), jnp.float32),
            pltpu.SemaphoreType.DMA,
            pltpu.SemaphoreType.DMA((N_COPIES,)),
            pltpu.SemaphoreType.DMA((N_COPIES,)),
        ],
        compiler_params=pltpu.CompilerParams(
            vmem_limit_bytes=28 * 1024 * 1024, collective_id=0, has_side_effects=True
        ),
        name="tail",
    )(attention, gain.reshape(1, D), in_hbm(tokens), w_out, head_t)


def local(
    tokens,
    w_query,
    query_bias,
    w_keyval,
    keyval_bias,
    w_out,
    attn_gain,
    final_norm_gain,
    head_weight,
    kv_pool,
    cache_len,
):
    new_kv, attention, w_out_v, head_v = attention_call(
        cache_len,
        tokens,
        w_query,
        w_keyval,
        query_bias,
        keyval_bias,
        attn_gain,
        kv_pool.reshape(POOL, KW),
        w_out,
        head_weight.T,
    )
    states, norms, top, logits_t = tail_call(attention, final_norm_gain, tokens, w_out_v, head_v)
    return (
        states,
        new_kv.reshape(ROWS, 1, KW),
        norms.reshape(REQ_DEV),
        top.reshape(2 * PAIR),
        logits_t.T,
    )


def solution(mesh):
    return jax.shard_map(
        local,
        mesh=mesh,
        in_specs=(
            P("req", None),
            P(None, "tp"),
            P("tp"),
            P(None, "tp"),
            P("tp"),
            P("tp", None),
            P(),
            P(),
            P(None, ("req", "tp")),
            P("req", "tp", None),
            P(),
        ),
        out_specs=(P("req", "tp"), P("req", "tp", None), P("req"), P(), P(None, ("req", "tp"))),
        check_vma=False,
    )
```

```python
import math

import jax
import jax.numpy as jnp
import numpy as np
from jax import lax
from jax.experimental import pallas as pl
from jax.experimental.pallas import tpu as pltpu
from jax.sharding import PartitionSpec as P

D = 5120
HD = 128
GROUP = 5
NEW = 24
SHORT = 256
LONG = 3072
REQ_DEV = 16
REQUESTS = 512
POOL = 26624
ROWS = REQ_DEV * NEW
QW = GROUP * HD
KW = 2 * HD
THETA = 1000000.0
EPS = 1e-06
NEG = -1e30

KC = 1024
NKC = D // KC
PC = 2048
NPC = POOL // PC
QR = 128
PER_STEP = 4
BATCH = 4
WIDE = (LONG - SHORT) // 2
VLOC = 594


def rope_tables():
    freq = np.float32(THETA) ** (-(np.arange(HD // 2, dtype=np.float32) * np.float32(2.0 / HD)))
    pos = np.concatenate([SHORT + np.arange(NEW), LONG + np.arange(NEW)]).astype(np.float32)
    ang = (pos[:, None] * freq[None, :].astype(np.float32)).astype(np.float64)
    cos = np.cos(ang).astype(np.float32)
    sin = np.sin(ang).astype(np.float32)
    return np.concatenate([cos, cos, -sin, sin], axis=1)


def attn_kernel(
    lens_hbm,
    tok_hbm,
    wq_hbm,
    wkv_hbm,
    qb_hbm,
    kvb_hbm,
    gain_hbm,
    cs_hbm,
    pool_hbm,
    wo_hbm,
    hw_hbm,
    newkv_ref,
    attn_ref,
    wo_ref,
    hw_ref,
    tok_v,
    w_v,
    pool_v,
    acc,
    ss,
    att_s,
    kv_s,
    q_s,
    m_s,
    l_s,
    o_s,
    lens_ref,
    start_ref,
    long_ref,
    qb_v,
    kvb_v,
    gain_v,
    cs_ref,
    tok_sem,
    wq_sem,
    wkv_sem,
    pool_sem,
    small_sem,
    tail_sem,
):
    def tok_copy(k):
        c = pl.ds(pl.multiple_of(k * KC, KC), KC)
        return pltpu.make_async_copy(tok_hbm.at[:, c], tok_v.at[:, c], tok_sem.at[k])

    def wq_copy(k):
        c = pl.ds(pl.multiple_of(k * KC, KC), KC)
        return pltpu.make_async_copy(wq_hbm.at[c, :], w_v.at[c, pl.ds(0, QW)], wq_sem.at[k])

    def wkv_copy(k):
        c = pl.ds(pl.multiple_of(k * KC, KC), KC)
        return pltpu.make_async_copy(wkv_hbm.at[c, :], w_v.at[c, pl.ds(QW, KW)], wkv_sem.at[k])

    def pool_copy(k):
        c = pl.ds(pl.multiple_of(k * PC, PC), PC)
        return pltpu.make_async_copy(pool_hbm.at[c, :], pool_v.at[c, :], pool_sem.at[k])

    smalls = [
        pltpu.make_async_copy(src, dst, small_sem.at[i])
        for i, (src, dst) in enumerate(
            ((gain_hbm, gain_v), (lens_hbm, lens_ref), (qb_hbm, qb_v), (kvb_hbm, kvb_v), (cs_hbm, cs_ref))
        )
    ]
    tails = [
        pltpu.make_async_copy(wo_hbm, wo_ref, tail_sem.at[0]),
        pltpu.make_async_copy(hw_hbm, hw_ref, tail_sem.at[1]),
    ]
    smalls[0].start()
    smalls[1].start()
    for k in range(NKC):
        tok_copy(k).start()
        wq_copy(k).start()
        wkv_copy(k).start()
    for c in smalls[2:]:
        c.start()
    ss[...] = jnp.zeros_like(ss)
    acc[...] = jnp.zeros_like(acc)
    base = lax.axis_index("req") * REQ_DEV
    smalls[1].wait()

    def place(r, carry):
        begin, n_long = carry
        length = lens_ref[base + r]
        start_ref[r] = begin
        long_ref[n_long] = r
        return begin + length, n_long + jnp.where(length > SHORT, 1, 0)

    _, n_long = lax.fori_loop(0, REQ_DEV, place, (jnp.int32(0), jnp.int32(0)))
    smalls[0].wait()

    for k in range(NKC):
        tok_copy(k).wait()
        wq_copy(k).wait()
        wkv_copy(k).wait()
        if k >= 1:
            for i in range(PER_STEP * (k - 1), min(PER_STEP * k, NPC)):
                pool_copy(i).start()
        c = slice(k * KC, (k + 1) * KC)
        x = tok_v[:, c].astype(jnp.float32)
        sq = x * x
        part = sq[:, 0:HD]
        for i in range(1, KC // HD):
            part = part + sq[:, i * HD : (i + 1) * HD]
        ss[...] += part
        xg = (x * gain_v[c].reshape(1, KC)).astype(jnp.bfloat16)
        acc[...] += jnp.dot(xg, w_v[c, :], preferred_element_type=jnp.float32)
    for c in smalls[2:]:
        c.wait()
    rstd = 1.0 / jnp.sqrt(jnp.sum(ss[...], axis=1, keepdims=True) * (1.0 / D) + EPS)
    ss[...] = jnp.broadcast_to(rstd, ss.shape)

    row = lax.broadcasted_iota(jnp.int32, (QR, HD), 0)
    col = lax.broadcasted_iota(jnp.int32, (QR, HD), 1)
    token = row
    for g in range(1, GROUP + 1):
        token = token - jnp.where(row >= g * NEW, NEW, 0)
    causal = (col <= token) & (col < NEW)
    scale = 1.0 / math.sqrt(HD)

    def wait_one(i, c):
        pool_copy(i).wait()
        return c

    def scores_of(q, k):
        return lax.dot_general(q, k, (((1,), (1,)), ((), ())), preferred_element_type=jnp.float32)

    def mix(p, v):
        return jnp.dot(p.astype(jnp.bfloat16), v, preferred_element_type=jnp.float32)

    def rows_of(r):
        return pl.ds(pl.multiple_of(r * NEW, 8), NEW)

    def store_heads(r, out):
        for g in range(GROUP):
            att_s[rows_of(r), g * HD : (g + 1) * HD] = out[g * NEW : (g + 1) * NEW, :]

    def batch(b, waited):
        ids = [b * BATCH + i for i in range(BATCH)]
        begins = [start_ref[r] for r in ids]
        need = (begins[-1] + SHORT + (PC - 1)) // PC
        lax.fori_loop(waited, need, wait_one, 0)
        fill = jnp.zeros((HD - NEW, HD), jnp.float32)
        qs, keys, values = [], [], []
        for r in ids:
            rows = rows_of(r)
            table = pl.ds(pl.multiple_of(jnp.where(lens_ref[base + r] > SHORT, NEW, 0), 8), NEW)
            cos = cs_ref[table, pl.ds(0, HD)]
            sin = cs_ref[table, pl.ds(HD, HD)]
            rs = ss[rows, :]

            def rope(v, cos=cos, sin=sin):
                return v * cos + pltpu.roll(v, HD // 2, 1) * sin

            heads = []
            for g in range(GROUP):
                c = slice(g * HD, (g + 1) * HD)
                heads.append(rope(acc[rows, c] * rs + qb_v[c].reshape(1, HD)) * scale)
            heads.append(jnp.zeros((QR - GROUP * NEW, HD), jnp.float32))
            qs.append(jnp.concatenate(heads, axis=0).astype(jnp.bfloat16))
            key = rope(acc[rows, QW : QW + HD] * rs + kvb_v[0:HD].reshape(1, HD))
            value = acc[rows, QW + HD : QW + KW] * rs + kvb_v[HD:KW].reshape(1, HD)
            kv_s[rows, 0:HD] = key
            kv_s[rows, HD:KW] = value
            keys.append(jnp.concatenate([key, fill], axis=0).astype(jnp.bfloat16))
            values.append(jnp.concatenate([value, fill], axis=0).astype(jnp.bfloat16))
        windows = [pl.ds(pl.multiple_of(x, SHORT), SHORT) for x in begins]
        old = [scores_of(q, pool_v[w, pl.ds(0, HD)]) for q, w in zip(qs, windows)]
        new = [jnp.where(causal, scores_of(q, k), NEG) for q, k in zip(qs, keys)]
        ms = [
            jnp.maximum(jnp.max(s, axis=1, keepdims=True), jnp.max(t, axis=1, keepdims=True))
            for s, t in zip(old, new)
        ]
        p_old = [jnp.exp(s - m) for s, m in zip(old, ms)]
        p_new = [jnp.exp(t - m) for t, m in zip(new, ms)]
        ls = [
            jnp.sum(p, axis=1, keepdims=True) + jnp.sum(u, axis=1, keepdims=True)
            for p, u in zip(p_old, p_new)
        ]
        outs = [
            mix(p, pool_v[w, pl.ds(HD, HD)]) + mix(u, v)
            for p, u, w, v in zip(p_old, p_new, windows, values)
        ]
        for i, r in enumerate(ids):
            q_s[r] = qs[i]
            m_s[r] = jnp.broadcast_to(ms[i], (QR, HD))
            l_s[r] = jnp.broadcast_to(ls[i], (QR, HD))
            o_s[r] = outs[i]
            store_heads(r, outs[i] / ls[i])
        return jnp.maximum(waited, need)

    waited = lax.fori_loop(0, REQ_DEV // BATCH - 1, batch, jnp.int32(0))
    for c in tails:
        c.start()
    waited = batch(REQ_DEV // BATCH - 1, waited)
    lax.fori_loop(waited, NPC, wait_one, 0)

    def longs(j, carry):
        ids = [long_ref[2 * j], long_ref[jnp.minimum(2 * j + 1, n_long - 1)]]
        begins = [pl.multiple_of(start_ref[r] + SHORT, SHORT) for r in ids]
        qs = [q_s[r] for r in ids]
        windows = [
            [pl.ds(pl.multiple_of(x + i * WIDE, HD), WIDE) for i in range((LONG - SHORT) // WIDE)] for x in begins
        ]
        scores = [[scores_of(q, pool_v[w, pl.ds(0, HD)]) for w in ws] for q, ws in zip(qs, windows)]
        outs = []
        for r, ws, parts in zip(ids, windows, scores):
            before = m_s[r][:, 0:1]
            m = before
            for s in parts:
                m = jnp.maximum(m, jnp.max(s, axis=1, keepdims=True))
            fade = jnp.exp(before - m)
            total = l_s[r][:, 0:1] * fade
            out = o_s[r] * fade
            for s, w in zip(parts, ws):
                p = jnp.exp(s - m)
                total = total + jnp.sum(p, axis=1, keepdims=True)
                out = out + mix(p, pool_v[w, pl.ds(HD, HD)])
            outs.append(out / total)
        for r, out in zip(ids, outs):
            store_heads(r, out)
        return carry

    lax.fori_loop(0, (n_long + 1) // 2, longs, 0)
    attn_ref[...] = att_s[...].astype(jnp.bfloat16)
    newkv_ref[...] = kv_s[...].astype(jnp.bfloat16)
    for c in tails:
        c.wait()


def in_hbm(a):
    return pltpu.with_memory_space_constraint(a, pltpu.HBM)


def attention_call(cache_len, tokens, w_query, w_keyval, query_bias, keyval_bias, gain, pool, w_out, head_t):
    vmem = pl.BlockSpec(memory_space=pltpu.VMEM)
    hbm = pl.BlockSpec(memory_space=pltpu.HBM)
    return pl.pallas_call(
        attn_kernel,
        out_shape=(
            jax.ShapeDtypeStruct((ROWS, KW), jnp.bfloat16),
            jax.ShapeDtypeStruct((ROWS, QW), jnp.bfloat16),
            jax.ShapeDtypeStruct((QW, D), jnp.bfloat16),
            jax.ShapeDtypeStruct((VLOC, D), jnp.bfloat16),
        ),
        in_specs=[hbm] * 11,
        out_specs=(vmem, vmem, vmem, vmem),
        scratch_shapes=[
            pltpu.VMEM((ROWS, D), jnp.bfloat16),
            pltpu.VMEM((D, QW + KW), jnp.bfloat16),
            pltpu.VMEM((POOL, KW), jnp.bfloat16),
            pltpu.VMEM((ROWS, QW + KW), jnp.float32),
            pltpu.VMEM((ROWS, HD), jnp.float32),
            pltpu.VMEM((ROWS, QW), jnp.float32),
            pltpu.VMEM((ROWS, KW), jnp.float32),
            pltpu.VMEM((REQ_DEV, QR, HD), jnp.bfloat16),
            pltpu.VMEM((REQ_DEV, QR, HD), jnp.float32),
            pltpu.VMEM((REQ_DEV, QR, HD), jnp.float32),
            pltpu.VMEM((REQ_DEV, QR, HD), jnp.float32),
            pltpu.SMEM((REQUESTS,), jnp.int32),
            pltpu.SMEM((REQ_DEV,), jnp.int32),
            pltpu.SMEM((REQ_DEV + 1,), jnp.int32),
            pltpu.VMEM((QW,), jnp.float32),
            pltpu.VMEM((KW,), jnp.float32),
            pltpu.VMEM((D,), jnp.float32),
            pltpu.VMEM((2 * NEW, 2 * HD), jnp.float32),
            pltpu.SemaphoreType.DMA((NKC,)),
            pltpu.SemaphoreType.DMA((NKC,)),
            pltpu.SemaphoreType.DMA((NKC,)),
            pltpu.SemaphoreType.DMA((NPC,)),
            pltpu.SemaphoreType.DMA((5,)),
            pltpu.SemaphoreType.DMA((2,)),
        ],
        compiler_params=pltpu.CompilerParams(vmem_limit_bytes=38 * 1024 * 1024),
        name="attend",
    )(
        in_hbm(cache_len),
        in_hbm(tokens),
        in_hbm(w_query),
        in_hbm(w_keyval),
        in_hbm(query_bias),
        in_hbm(keyval_bias),
        in_hbm(gain),
        in_hbm(jnp.asarray(rope_tables())),
        in_hbm(pool),
        in_hbm(w_out),
        in_hbm(head_t),
    )


CHUNKS = 4
CROWS = ROWS // CHUNKS
HROWS = CROWS // 2
TP = 4
WIDTH = D // TP
HALF = D // 2
QUART = HALF // 2
PAIR = 256
MESH = pl.DeviceIdType.MESH
N_COPIES = 124


def tail_kernel(
    attn_ref,
    gain_ref,
    tok_hbm,
    wo_ref,
    hw_ref,
    states_ref,
    norms_ref,
    max_ref,
    logits_ref,
    tok_v,
    own_state,
    gathered,
    last_out,
    last_in,
    far_out,
    far_l,
    far_r,
    part_r,
    part_l,
    part_own,
    near_out_r,
    near_out_l,
    near_in_l,
    near_in_r,
    mx,
    mx_in,
    tok_sem,
    send_sem,
    recv_sem,
):
    req = lax.axis_index("req")
    y = lax.axis_index("tp")
    core = lax.rem(req, 2)
    x = lax.rem(req // 2, 4)
    z = req // 8
    right, left, opp = lax.rem(y + 1, TP), lax.rem(y + 3, TP), lax.rem(y + 2, TP)

    def at(dx=0, dz=0, dc=0, dy=0):
        xx, zz, cc = lax.rem(x + dx, 4), lax.rem(z + dz, 4), lax.rem(core + dc, 2)
        return {"req": (zz * 4 + xx) * 2 + cc, "tp": lax.rem(y + dy, TP)}

    plane = [{"dx": i, "dz": j} for i in range(4) for j in range(4) if i or j]
    column = [{"dy": i, "dc": j} for i in range(4) for j in range(2) if i or j]
    peers = [at(**move) for move in plane + column]

    def wide(d):
        return pl.ds(pl.multiple_of(d * WIDTH, WIDTH), WIDTH)

    tok_copy = pltpu.make_async_copy(tok_hbm.at[:, wide(y)], tok_v, tok_sem)
    tok_copy.start()

    barrier = pltpu.get_barrier_semaphore()
    for peer in peers:
        pl.semaphore_signal(barrier, inc=1, device_id=peer, device_id_type=MESH)

    copies = {}

    def send(name, src, dst, device):
        i = len(copies)
        copies[name] = pltpu.make_async_remote_copy(
            src_ref=src,
            dst_ref=dst,
            send_sem=send_sem.at[i],
            recv_sem=recv_sem.at[i],
            device_id=device,
            device_id_type=MESH,
        )
        copies[name].start()

    def got(name):
        copies[name].wait_recv()

    pick_row = lax.broadcasted_iota(jnp.int32, (REQ_DEV, ROWS), 0)
    pick_col = lax.broadcasted_iota(jnp.int32, (REQ_DEV, ROWS), 1)
    pick = (pick_col == pick_row * NEW + (NEW - 1)).astype(jnp.bfloat16)
    attn_last = jnp.dot(pick, attn_ref[...], preferred_element_type=jnp.float32).astype(jnp.bfloat16)

    def project(dy, out_ref):
        out_ref[...] = jnp.dot(
            attn_ref[...], wo_ref[:, wide(lax.rem(y + dy, TP))], preferred_element_type=jnp.float32
        ).astype(out_ref.dtype)

    def far_send(c):
        r = c * CROWS
        send(("far", c, 1), far_out.at[r : r + HROWS], far_l.at[c], at(dy=1))
        send(("far", c, 3), far_out.at[r + HROWS : r + CROWS], far_r.at[c], at(dy=3))

    order = ((2, 0), (1, 1), (3, 2))
    for dy, i in order:
        last_out[i] = jnp.dot(
            attn_last, wo_ref[:, wide(lax.rem(y + dy, TP))], preferred_element_type=jnp.float32
        ).astype(jnp.bfloat16)
    project(2, far_out)
    pl.semaphore_wait(barrier, len(peers))
    for dy, i in order:
        send(("last", dy), last_out.at[i], last_in.at[i], at(dy=dy))
    far_send(0)
    own_last = jnp.dot(attn_last, wo_ref[:, wide(y)], preferred_element_type=jnp.float32)
    tok_copy.wait()
    own_last = own_last + jnp.dot(pick, tok_v[...], preferred_element_type=jnp.float32)
    project(1, part_r)
    for dy, i in order:
        got(("last", dy))
        own_last = own_last + last_in[i].astype(jnp.float32)
    own_rows = pl.ds(pl.multiple_of(req * REQ_DEV, REQ_DEV), REQ_DEV)
    own_state[:, wide(y)] = own_last.astype(jnp.bfloat16)
    for dy in (1, 3, 2):
        block = own_state.at[:, wide(y)]
        send(("slice", dy), block, block, at(dy=dy))
    for c in range(1, CHUNKS):
        far_send(c)
    project(3, part_l)
    for dy in (1, 3, 2):
        got(("slice", dy))
    own = own_state[...].astype(jnp.float32)
    own_norm = jnp.sqrt(jnp.sum(own * own, axis=1, keepdims=True) * (1.0 / D) + EPS)
    gathered[own_rows, :] = (own / own_norm * gain_ref[...]).astype(jnp.bfloat16)

    def device(half, df=0, ds=0):
        return at(dx=df, dz=ds) if half == 0 else at(dx=ds, dz=df)

    def piece(half, df, ds, part=None):
        d = device(half, df, ds)["req"]
        rows = pl.ds(pl.multiple_of(d * REQ_DEV, REQ_DEV), REQ_DEV)
        start, width = half * HALF, HALF
        if part is not None:
            start, width = start + part * QUART, QUART
        return gathered.at[rows, start : start + width]

    def push(name, half, df, ds, to, part=None):
        block = piece(half, df, ds, part)
        send((name, half, df, ds, part), block, block, to)

    def spread(half, k):
        for side in (1, 3):
            block = piece(half, k, 0)
            send(("second", half, k, side), block, block, device(half, 0, side))

    def sibling(half, df, ds):
        push("sib", half, df, ds, at(dc=1))

    for half in (0, 1):
        for side in (1, 3):
            block = piece(half, 0, 0)
            send(("first", half, side), block, block, device(half, side, 0))
    for half in (0, 1):
        spread(half, 0)
    for half in (0, 1):
        sibling(half, 0, 0)

    eye_row = lax.broadcasted_iota(jnp.int32, (REQ_DEV, REQ_DEV), 0)
    eye_col = lax.broadcasted_iota(jnp.int32, (REQ_DEV, REQ_DEV), 1)
    norms_ref[...] = jnp.sum(jnp.where(eye_row == eye_col, own_norm, 0.0), axis=0, keepdims=True)

    def near_step(c):
        r = c * CROWS
        got(("far", c, 1))
        near_out_r[c, 0:HROWS] = (part_r[r : r + HROWS] + far_l[c].astype(jnp.float32)).astype(jnp.bfloat16)
        near_out_r[c, HROWS:CROWS] = part_r[r + HROWS : r + CROWS].astype(jnp.bfloat16)
        send(("near", c, 1), near_out_r.at[c], near_in_l.at[c], at(dy=1))
        got(("far", c, 3))
        near_out_l[c, 0:HROWS] = part_l[r : r + HROWS].astype(jnp.bfloat16)
        near_out_l[c, HROWS:CROWS] = (part_l[r + HROWS : r + CROWS] + far_r[c].astype(jnp.float32)).astype(jnp.bfloat16)
        send(("near", c, 3), near_out_l.at[c], near_in_r.at[c], at(dy=3))

    def relay_second(half, k):
        for side, part, ds in ((1, 0, 3), (3, 1, 1)):
            got(("second", half, k, side))
            block = piece(half, k, ds, part)
            send(("third", half, k, side), block, block, device(half, 0, side))
            sibling(half, k, ds)

    def finish_second(half, k):
        for side in (1, 3):
            got(("third", half, k, side))
        sibling(half, k, 2)

    def logits_of(pair, shifts):
        for dz in shifts:
            for dx in range(4):
                got(("sib", 0, dx, dz, None))
                got(("sib", 1, dz, dx, None))
        rows = pl.ds(pl.multiple_of(pair * PAIR, PAIR), PAIR)
        out = lax.dot_general(
            hw_ref[...], gathered[rows, :], (((1,), (1,)), ((), ())), preferred_element_type=jnp.float32
        )
        logits_ref[:, rows] = out
        mx[0, pl.ds(pair, 1), :] = jnp.max(out, axis=0, keepdims=True)

    project(0, part_own)
    for side, part, df in ((1, 0, 3), (3, 1, 1)):
        for half in (0, 1):
            got(("first", half, side))
            block = piece(half, df, 0, part)
            send(("relay", half, side), block, block, device(half, side, 0))
    for half in (0, 1):
        spread(half, 3)
        spread(half, 1)
    for half in (0, 1):
        sibling(half, 3, 0)
        sibling(half, 1, 0)
    near_step(0)
    for half in (0, 1):
        for side in (1, 3):
            got(("relay", half, side))
        spread(half, 2)
    for half in (0, 1):
        relay_second(half, 0)
    for half in (0, 1):
        sibling(half, 2, 0)
    near_step(1)
    for k in (3, 1):
        for half in (0, 1):
            relay_second(half, k)
    near_step(2)
    for half in (0, 1):
        finish_second(half, 0)
    for half in (0, 1):
        relay_second(half, 2)
    near_step(3)
    for k in (3, 1):
        for half in (0, 1):
            finish_second(half, k)
    mine, other = z // 2, 1 - z // 2

    for half in (0, 1):
        finish_second(half, 2)
    logits_of(mine, (0, 1, 3))
    logits_of(other, (2,))

    def spread_max(stage, moves):
        for i, move in enumerate(moves):
            send(("max", stage, i), mx.at[stage], mx_in.at[stage, i], at(**move))

    def take_max(stage, moves):
        m = mx[stage]
        for i in range(len(moves)):
            got(("max", stage, i))
            m = jnp.maximum(m, mx_in[stage, i])
        return m

    spread_max(0, plane)
    mx[1] = take_max(0, plane)
    spread_max(1, column)

    for c in range(CHUNKS):
        r = slice(c * CROWS, (c + 1) * CROWS)
        got(("near", c, 1))
        got(("near", c, 3))
        total = tok_v[r].astype(jnp.float32) + part_own[r] + near_in_l[c].astype(jnp.float32)
        states_ref[r] = (total + near_in_r[c].astype(jnp.float32)).astype(jnp.bfloat16)
    top = take_max(1, column)
    for i in range(4):
        h = HD * (i % 2)
        max_ref[i : i + 1, :] = top[i // 2 : i // 2 + 1, h : h + HD]
    for c in copies.values():
        c.wait_send()


def tail_call(attention, gain, tokens, w_out, head_t):
    vmem = pl.BlockSpec(memory_space=pltpu.VMEM)
    hbm = pl.BlockSpec(memory_space=pltpu.HBM)
    half = jnp.bfloat16
    return pl.pallas_call(
        tail_kernel,
        out_shape=(
            jax.ShapeDtypeStruct((ROWS, WIDTH), half),
            jax.ShapeDtypeStruct((1, REQ_DEV), jnp.float32),
            jax.ShapeDtypeStruct((4, HD), jnp.float32),
            jax.ShapeDtypeStruct((VLOC, 2 * PAIR), jnp.float32),
        ),
        in_specs=[vmem, vmem, hbm, vmem, vmem],
        out_specs=(vmem, vmem, vmem, vmem),
        scratch_shapes=[
            pltpu.VMEM((ROWS, WIDTH), half),
            pltpu.VMEM((REQ_DEV, D), half),
            pltpu.VMEM((2 * PAIR, D), half),
            pltpu.VMEM((3, REQ_DEV, WIDTH), half),
            pltpu.VMEM((3, REQ_DEV, WIDTH), half),
            pltpu.VMEM((ROWS, WIDTH), half),
            pltpu.VMEM((CHUNKS, HROWS, WIDTH), half),
            pltpu.VMEM((CHUNKS, HROWS, WIDTH), half),
            pltpu.VMEM((ROWS, WIDTH), jnp.float32),
            pltpu.VMEM((ROWS, WIDTH), jnp.float32),
            pltpu.VMEM((ROWS, WIDTH), jnp.float32),
            pltpu.VMEM((CHUNKS, CROWS, WIDTH), half),
            pltpu.VMEM((CHUNKS, CROWS, WIDTH), half),
            pltpu.VMEM((CHUNKS, CROWS, WIDTH), half),
            pltpu.VMEM((CHUNKS, CROWS, WIDTH), half),
            pltpu.VMEM((2, 2, PAIR), jnp.float32),
            pltpu.VMEM((2, 15, 2, PAIR), jnp.float32),
            pltpu.SemaphoreType.DMA,
            pltpu.SemaphoreType.DMA((N_COPIES,)),
            pltpu.SemaphoreType.DMA((N_COPIES,)),
        ],
        compiler_params=pltpu.CompilerParams(
            vmem_limit_bytes=28 * 1024 * 1024, collective_id=0, has_side_effects=True
        ),
        name="tail",
    )(attention, gain.reshape(1, D), in_hbm(tokens), w_out, head_t)


def out_kernel(*refs):
    n = len(refs) // 2
    sems = refs[-1]
    moves = [pltpu.make_async_copy(refs[i], refs[n + i], sems.at[i]) for i in range(n)]
    for m in moves:
        m.start()
    for m in moves:
        m.wait()


def out_call(*arrays):
    return pl.pallas_call(
        out_kernel,
        out_shape=tuple(jax.ShapeDtypeStruct(a.shape, a.dtype) for a in arrays),
        in_specs=[pl.BlockSpec(memory_space=pltpu.VMEM)] * len(arrays),
        out_specs=tuple(pl.BlockSpec(memory_space=pltpu.HBM) for _ in arrays),
        scratch_shapes=[pltpu.SemaphoreType.DMA((len(arrays),))],
        compiler_params=pltpu.CompilerParams(vmem_limit_bytes=4 * 1024 * 1024),
        name="write",
    )(*arrays)


def local(
    tokens,
    w_query,
    query_bias,
    w_keyval,
    keyval_bias,
    w_out,
    attn_gain,
    final_norm_gain,
    head_weight,
    kv_pool,
    cache_len,
):
    new_kv, attention, w_out_v, head_v = attention_call(
        cache_len,
        tokens,
        w_query,
        w_keyval,
        query_bias,
        keyval_bias,
        attn_gain,
        kv_pool.reshape(POOL, KW),
        w_out,
        head_weight.T,
    )
    states, norms, top, logits_t = out_call(*tail_call(attention, final_norm_gain, tokens, w_out_v, head_v))
    return (
        states,
        new_kv.reshape(ROWS, 1, KW),
        norms.reshape(REQ_DEV),
        top.reshape(2 * PAIR),
        logits_t.T,
    )


def solution(mesh):
    return jax.shard_map(
        local,
        mesh=mesh,
        in_specs=(
            P("req", None),
            P(None, "tp"),
            P("tp"),
            P(None, "tp"),
            P("tp"),
            P("tp", None),
            P(),
            P(),
            P(None, ("req", "tp")),
            P("req", "tp", None),
            P(),
        ),
        out_specs=(P("req", "tp"), P("req", "tp", None), P("req"), P(), P(None, ("req", "tp"))),
        check_vma=False,
    )
```

```python
import math

import jax
import jax.numpy as jnp
import numpy as np
from jax import lax
from jax.experimental import pallas as pl
from jax.experimental.pallas import tpu as pltpu
from jax.sharding import PartitionSpec as P

D = 5120
HD = 128
GROUP = 5
NEW = 24
SHORT = 256
LONG = 3072
REQ_DEV = 16
REQUESTS = 512
POOL = 26624
ROWS = REQ_DEV * NEW
QW = GROUP * HD
KW = 2 * HD
THETA = 1000000.0
EPS = 1e-06
NEG = -1e30

KC = 1024
NKC = D // KC
PC = 2048
NPC = POOL // PC
QR = 128
AHEAD = 3
PER_STEP = 5
BATCH = 4
WIDE = (LONG - SHORT) // 2
VLOC = 594


def rope_tables():
    freq = np.float32(THETA) ** (-(np.arange(HD // 2, dtype=np.float32) * np.float32(2.0 / HD)))
    pos = np.concatenate([SHORT + np.arange(NEW), LONG + np.arange(NEW)]).astype(np.float32)
    ang = (pos[:, None] * freq[None, :].astype(np.float32)).astype(np.float64)
    cos = np.cos(ang).astype(np.float32)
    sin = np.sin(ang).astype(np.float32)
    return np.concatenate([cos, cos, -sin, sin], axis=1)


def attn_kernel(
    lens_hbm,
    tok_hbm,
    wq_hbm,
    wkv_hbm,
    qb_hbm,
    kvb_hbm,
    gain_hbm,
    cs_hbm,
    pool_hbm,
    wo_hbm,
    hw_hbm,
    newkv_ref,
    attn_ref,
    wo_ref,
    hw_ref,
    tok_v,
    w_v,
    pool_v,
    acc,
    ss,
    att_s,
    kv_s,
    q_s,
    m_s,
    l_s,
    o_s,
    lens_ref,
    start_ref,
    long_ref,
    qb_v,
    kvb_v,
    gain_v,
    cs_ref,
    tok_sem,
    wq_sem,
    wkv_sem,
    pool_sem,
    small_sem,
    tail_sem,
):
    def tok_copy(k):
        c = pl.ds(pl.multiple_of(k * KC, KC), KC)
        return pltpu.make_async_copy(tok_hbm.at[:, c], tok_v.at[:, c], tok_sem.at[k])

    def wq_copy(k):
        c = pl.ds(pl.multiple_of(k * KC, KC), KC)
        return pltpu.make_async_copy(wq_hbm.at[c, :], w_v.at[c, pl.ds(0, QW)], wq_sem.at[k])

    def wkv_copy(k):
        c = pl.ds(pl.multiple_of(k * KC, KC), KC)
        return pltpu.make_async_copy(wkv_hbm.at[c, :], w_v.at[c, pl.ds(QW, KW)], wkv_sem.at[k])

    def pool_copy(k):
        c = pl.ds(pl.multiple_of(k * PC, PC), PC)
        return pltpu.make_async_copy(pool_hbm.at[c, :], pool_v.at[c, :], pool_sem.at[k])

    smalls = [
        pltpu.make_async_copy(src, dst, small_sem.at[i])
        for i, (src, dst) in enumerate(
            ((gain_hbm, gain_v), (lens_hbm, lens_ref), (qb_hbm, qb_v), (kvb_hbm, kvb_v), (cs_hbm, cs_ref))
        )
    ]
    tails = [
        pltpu.make_async_copy(wo_hbm, wo_ref, tail_sem.at[0]),
        pltpu.make_async_copy(hw_hbm, hw_ref, tail_sem.at[1]),
    ]
    smalls[0].start()
    smalls[1].start()
    def feed(k):
        tok_copy(k).start()
        wq_copy(k).start()
        wkv_copy(k).start()

    for k in range(AHEAD):
        feed(k)
    for c in smalls[2:]:
        c.start()
    ss[...] = jnp.zeros_like(ss)
    acc[...] = jnp.zeros_like(acc)
    base = lax.axis_index("req") * REQ_DEV
    smalls[1].wait()

    def place(r, carry):
        begin, n_long = carry
        length = lens_ref[base + r]
        start_ref[r] = begin
        long_ref[n_long] = r
        return begin + length, n_long + jnp.where(length > SHORT, 1, 0)

    _, n_long = lax.fori_loop(0, REQ_DEV, place, (jnp.int32(0), jnp.int32(0)))
    smalls[0].wait()

    for k in range(NKC):
        tok_copy(k).wait()
        wq_copy(k).wait()
        wkv_copy(k).wait()
        if k + AHEAD < NKC:
            feed(k + AHEAD)
        else:
            first = k + AHEAD - NKC
            for i in range(PER_STEP * first, min(PER_STEP * (first + 1), NPC)):
                pool_copy(i).start()
        c = slice(k * KC, (k + 1) * KC)
        x = tok_v[:, c].astype(jnp.float32)
        sq = x * x
        part = sq[:, 0:HD]
        for i in range(1, KC // HD):
            part = part + sq[:, i * HD : (i + 1) * HD]
        ss[...] += part
        xg = (x * gain_v[c].reshape(1, KC)).astype(jnp.bfloat16)
        acc[...] += jnp.dot(xg, w_v[c, :], preferred_element_type=jnp.float32)
    for c in smalls[2:]:
        c.wait()
    rstd = 1.0 / jnp.sqrt(jnp.sum(ss[...], axis=1, keepdims=True) * (1.0 / D) + EPS)
    ss[...] = jnp.broadcast_to(rstd, ss.shape)

    row = lax.broadcasted_iota(jnp.int32, (QR, HD), 0)
    col = lax.broadcasted_iota(jnp.int32, (QR, HD), 1)
    token = row
    for g in range(1, GROUP + 1):
        token = token - jnp.where(row >= g * NEW, NEW, 0)
    causal = (col <= token) & (col < NEW)
    scale = 1.0 / math.sqrt(HD)

    def wait_one(i, c):
        pool_copy(i).wait()
        return c

    def scores_of(q, k):
        return lax.dot_general(q, k, (((1,), (1,)), ((), ())), preferred_element_type=jnp.float32)

    def mix(p, v):
        return jnp.dot(p.astype(jnp.bfloat16), v, preferred_element_type=jnp.float32)

    def rows_of(r):
        return pl.ds(pl.multiple_of(r * NEW, 8), NEW)

    def store_heads(r, out):
        for g in range(GROUP):
            att_s[rows_of(r), g * HD : (g + 1) * HD] = out[g * NEW : (g + 1) * NEW, :]

    def batch(b, waited):
        ids = [b * BATCH + i for i in range(BATCH)]
        begins = [start_ref[r] for r in ids]
        need = (begins[-1] + SHORT + (PC - 1)) // PC
        lax.fori_loop(waited, need, wait_one, 0)
        fill = jnp.zeros((HD - NEW, HD), jnp.float32)
        qs, keys, values = [], [], []
        for r in ids:
            rows = rows_of(r)
            table = pl.ds(pl.multiple_of(jnp.where(lens_ref[base + r] > SHORT, NEW, 0), 8), NEW)
            cos = cs_ref[table, pl.ds(0, HD)]
            sin = cs_ref[table, pl.ds(HD, HD)]
            rs = ss[rows, :]

            def rope(v, cos=cos, sin=sin):
                return v * cos + pltpu.roll(v, HD // 2, 1) * sin

            heads = []
            for g in range(GROUP):
                c = slice(g * HD, (g + 1) * HD)
                heads.append(rope(acc[rows, c] * rs + qb_v[c].reshape(1, HD)) * scale)
            heads.append(jnp.zeros((QR - GROUP * NEW, HD), jnp.float32))
            qs.append(jnp.concatenate(heads, axis=0).astype(jnp.bfloat16))
            key = rope(acc[rows, QW : QW + HD] * rs + kvb_v[0:HD].reshape(1, HD))
            value = acc[rows, QW + HD : QW + KW] * rs + kvb_v[HD:KW].reshape(1, HD)
            kv_s[rows, 0:HD] = key
            kv_s[rows, HD:KW] = value
            keys.append(jnp.concatenate([key, fill], axis=0).astype(jnp.bfloat16))
            values.append(jnp.concatenate([value, fill], axis=0).astype(jnp.bfloat16))
        windows = [pl.ds(pl.multiple_of(x, SHORT), SHORT) for x in begins]
        old = [scores_of(q, pool_v[w, pl.ds(0, HD)]) for q, w in zip(qs, windows)]
        new = [jnp.where(causal, scores_of(q, k), NEG) for q, k in zip(qs, keys)]
        ms = [
            jnp.maximum(jnp.max(s, axis=1, keepdims=True), jnp.max(t, axis=1, keepdims=True))
            for s, t in zip(old, new)
        ]
        p_old = [jnp.exp(s - m) for s, m in zip(old, ms)]
        p_new = [jnp.exp(t - m) for t, m in zip(new, ms)]
        ls = [
            jnp.sum(p, axis=1, keepdims=True) + jnp.sum(u, axis=1, keepdims=True)
            for p, u in zip(p_old, p_new)
        ]
        outs = [
            mix(p, pool_v[w, pl.ds(HD, HD)]) + mix(u, v)
            for p, u, w, v in zip(p_old, p_new, windows, values)
        ]
        for i, r in enumerate(ids):
            q_s[r] = qs[i]
            m_s[r] = jnp.broadcast_to(ms[i], (QR, HD))
            l_s[r] = jnp.broadcast_to(ls[i], (QR, HD))
            o_s[r] = outs[i]
            store_heads(r, outs[i] / ls[i])
        return jnp.maximum(waited, need)

    waited = lax.fori_loop(0, REQ_DEV // BATCH - 1, batch, jnp.int32(0))
    for c in tails:
        c.start()
    waited = batch(REQ_DEV // BATCH - 1, waited)
    lax.fori_loop(waited, NPC, wait_one, 0)

    def longs(j, carry):
        ids = [long_ref[2 * j], long_ref[jnp.minimum(2 * j + 1, n_long - 1)]]
        begins = [pl.multiple_of(start_ref[r] + SHORT, SHORT) for r in ids]
        qs = [q_s[r] for r in ids]
        windows = [
            [pl.ds(pl.multiple_of(x + i * WIDE, HD), WIDE) for i in range((LONG - SHORT) // WIDE)] for x in begins
        ]
        scores = [[scores_of(q, pool_v[w, pl.ds(0, HD)]) for w in ws] for q, ws in zip(qs, windows)]
        outs = []
        for r, ws, parts in zip(ids, windows, scores):
            before = m_s[r][:, 0:1]
            m = before
            for s in parts:
                m = jnp.maximum(m, jnp.max(s, axis=1, keepdims=True))
            fade = jnp.exp(before - m)
            total = l_s[r][:, 0:1] * fade
            out = o_s[r] * fade
            for s, w in zip(parts, ws):
                p = jnp.exp(s - m)
                total = total + jnp.sum(p, axis=1, keepdims=True)
                out = out + mix(p, pool_v[w, pl.ds(HD, HD)])
            outs.append(out / total)
        for r, out in zip(ids, outs):
            store_heads(r, out)
        return carry

    lax.fori_loop(0, (n_long + 1) // 2, longs, 0)
    attn_ref[...] = att_s[...].astype(jnp.bfloat16)
    newkv_ref[...] = kv_s[...].astype(jnp.bfloat16)
    for c in tails:
        c.wait()


def in_hbm(a):
    return pltpu.with_memory_space_constraint(a, pltpu.HBM)


def attention_call(cache_len, tokens, w_query, w_keyval, query_bias, keyval_bias, gain, pool, w_out, head_t):
    vmem = pl.BlockSpec(memory_space=pltpu.VMEM)
    hbm = pl.BlockSpec(memory_space=pltpu.HBM)
    return pl.pallas_call(
        attn_kernel,
        out_shape=(
            jax.ShapeDtypeStruct((ROWS, KW), jnp.bfloat16),
            jax.ShapeDtypeStruct((ROWS, QW), jnp.bfloat16),
            jax.ShapeDtypeStruct((QW, D), jnp.bfloat16),
            jax.ShapeDtypeStruct((VLOC, D), jnp.bfloat16),
        ),
        in_specs=[hbm] * 11,
        out_specs=(vmem, vmem, vmem, vmem),
        scratch_shapes=[
            pltpu.VMEM((ROWS, D), jnp.bfloat16),
            pltpu.VMEM((D, QW + KW), jnp.bfloat16),
            pltpu.VMEM((POOL, KW), jnp.bfloat16),
            pltpu.VMEM((ROWS, QW + KW), jnp.float32),
            pltpu.VMEM((ROWS, HD), jnp.float32),
            pltpu.VMEM((ROWS, QW), jnp.float32),
            pltpu.VMEM((ROWS, KW), jnp.float32),
            pltpu.VMEM((REQ_DEV, QR, HD), jnp.bfloat16),
            pltpu.VMEM((REQ_DEV, QR, HD), jnp.float32),
            pltpu.VMEM((REQ_DEV, QR, HD), jnp.float32),
            pltpu.VMEM((REQ_DEV, QR, HD), jnp.float32),
            pltpu.SMEM((REQUESTS,), jnp.int32),
            pltpu.SMEM((REQ_DEV,), jnp.int32),
            pltpu.SMEM((REQ_DEV + 1,), jnp.int32),
            pltpu.VMEM((QW,), jnp.float32),
            pltpu.VMEM((KW,), jnp.float32),
            pltpu.VMEM((D,), jnp.float32),
            pltpu.VMEM((2 * NEW, 2 * HD), jnp.float32),
            pltpu.SemaphoreType.DMA((NKC,)),
            pltpu.SemaphoreType.DMA((NKC,)),
            pltpu.SemaphoreType.DMA((NKC,)),
            pltpu.SemaphoreType.DMA((NPC,)),
            pltpu.SemaphoreType.DMA((5,)),
            pltpu.SemaphoreType.DMA((2,)),
        ],
        compiler_params=pltpu.CompilerParams(vmem_limit_bytes=38 * 1024 * 1024),
        name="attend",
    )(
        in_hbm(cache_len),
        in_hbm(tokens),
        in_hbm(w_query),
        in_hbm(w_keyval),
        in_hbm(query_bias),
        in_hbm(keyval_bias),
        in_hbm(gain),
        in_hbm(jnp.asarray(rope_tables())),
        in_hbm(pool),
        in_hbm(w_out),
        in_hbm(head_t),
    )


CHUNKS = 4
CROWS = ROWS // CHUNKS
HROWS = CROWS // 2
TP = 4
WIDTH = D // TP
HALF = D // 2
QUART = HALF // 2
PAIR = 256
MESH = pl.DeviceIdType.MESH
N_COPIES = 124


def tail_kernel(
    attn_ref,
    gain_ref,
    tok_hbm,
    wo_ref,
    hw_ref,
    states_ref,
    norms_ref,
    max_ref,
    logits_ref,
    tok_v,
    own_state,
    gathered,
    last_out,
    last_in,
    far_out,
    far_l,
    far_r,
    part_r,
    part_l,
    part_own,
    near_out_r,
    near_out_l,
    near_in_l,
    near_in_r,
    mx,
    mx_in,
    tok_sem,
    send_sem,
    recv_sem,
):
    req = lax.axis_index("req")
    y = lax.axis_index("tp")
    core = lax.rem(req, 2)
    x = lax.rem(req // 2, 4)
    z = req // 8
    right, left, opp = lax.rem(y + 1, TP), lax.rem(y + 3, TP), lax.rem(y + 2, TP)

    def at(dx=0, dz=0, dc=0, dy=0):
        xx, zz, cc = lax.rem(x + dx, 4), lax.rem(z + dz, 4), lax.rem(core + dc, 2)
        return {"req": (zz * 4 + xx) * 2 + cc, "tp": lax.rem(y + dy, TP)}

    plane = [{"dx": i, "dz": j} for i in range(4) for j in range(4) if i or j]
    column = [{"dy": i, "dc": j} for i in range(4) for j in range(2) if i or j]
    peers = [at(**move) for move in plane + column]

    def wide(d):
        return pl.ds(pl.multiple_of(d * WIDTH, WIDTH), WIDTH)

    tok_copy = pltpu.make_async_copy(tok_hbm.at[:, wide(y)], tok_v, tok_sem)
    tok_copy.start()

    barrier = pltpu.get_barrier_semaphore()
    for peer in peers:
        pl.semaphore_signal(barrier, inc=1, device_id=peer, device_id_type=MESH)

    copies = {}

    def send(name, src, dst, device):
        i = len(copies)
        copies[name] = pltpu.make_async_remote_copy(
            src_ref=src,
            dst_ref=dst,
            send_sem=send_sem.at[i],
            recv_sem=recv_sem.at[i],
            device_id=device,
            device_id_type=MESH,
        )
        copies[name].start()

    def got(name):
        copies[name].wait_recv()

    pick_row = lax.broadcasted_iota(jnp.int32, (REQ_DEV, ROWS), 0)
    pick_col = lax.broadcasted_iota(jnp.int32, (REQ_DEV, ROWS), 1)
    pick = (pick_col == pick_row * NEW + (NEW - 1)).astype(jnp.bfloat16)
    attn_last = jnp.dot(pick, attn_ref[...], preferred_element_type=jnp.float32).astype(jnp.bfloat16)

    def project(dy, out_ref):
        out_ref[...] = jnp.dot(
            attn_ref[...], wo_ref[:, wide(lax.rem(y + dy, TP))], preferred_element_type=jnp.float32
        ).astype(out_ref.dtype)

    def far_send(c):
        r = c * CROWS
        send(("far", c, 1), far_out.at[r : r + HROWS], far_l.at[c], at(dy=1))
        send(("far", c, 3), far_out.at[r + HROWS : r + CROWS], far_r.at[c], at(dy=3))

    order = ((2, 0), (1, 1), (3, 2))
    for dy, i in order:
        last_out[i] = jnp.dot(
            attn_last, wo_ref[:, wide(lax.rem(y + dy, TP))], preferred_element_type=jnp.float32
        ).astype(jnp.bfloat16)
    project(2, far_out)
    pl.semaphore_wait(barrier, len(peers))
    for dy, i in order:
        send(("last", dy), last_out.at[i], last_in.at[i], at(dy=dy))
    far_send(0)
    own_last = jnp.dot(attn_last, wo_ref[:, wide(y)], preferred_element_type=jnp.float32)
    tok_copy.wait()
    own_last = own_last + jnp.dot(pick, tok_v[...], preferred_element_type=jnp.float32)
    project(1, part_r)
    for dy, i in order:
        got(("last", dy))
        own_last = own_last + last_in[i].astype(jnp.float32)
    own_rows = pl.ds(pl.multiple_of(req * REQ_DEV, REQ_DEV), REQ_DEV)
    own_state[:, wide(y)] = own_last.astype(jnp.bfloat16)
    for dy in (1, 3, 2):
        block = own_state.at[:, wide(y)]
        send(("slice", dy), block, block, at(dy=dy))
    for c in range(1, CHUNKS):
        far_send(c)
    project(3, part_l)
    for dy in (1, 3, 2):
        got(("slice", dy))
    own = own_state[...].astype(jnp.float32)
    own_norm = jnp.sqrt(jnp.sum(own * own, axis=1, keepdims=True) * (1.0 / D) + EPS)
    gathered[own_rows, :] = (own / own_norm * gain_ref[...]).astype(jnp.bfloat16)

    def device(half, df=0, ds=0):
        return at(dx=df, dz=ds) if half == 0 else at(dx=ds, dz=df)

    def piece(half, df, ds, part=None):
        d = device(half, df, ds)["req"]
        rows = pl.ds(pl.multiple_of(d * REQ_DEV, REQ_DEV), REQ_DEV)
        start, width = half * HALF, HALF
        if part is not None:
            start, width = start + part * QUART, QUART
        return gathered.at[rows, start : start + width]

    def push(name, half, df, ds, to, part=None):
        block = piece(half, df, ds, part)
        send((name, half, df, ds, part), block, block, to)

    def spread(half, k):
        for side in (1, 3):
            block = piece(half, k, 0)
            send(("second", half, k, side), block, block, device(half, 0, side))

    def sibling(half, df, ds):
        push("sib", half, df, ds, at(dc=1))

    for half in (0, 1):
        for side in (1, 3):
            block = piece(half, 0, 0)
            send(("first", half, side), block, block, device(half, side, 0))
    for half in (0, 1):
        spread(half, 0)
    for half in (0, 1):
        sibling(half, 0, 0)

    eye_row = lax.broadcasted_iota(jnp.int32, (REQ_DEV, REQ_DEV), 0)
    eye_col = lax.broadcasted_iota(jnp.int32, (REQ_DEV, REQ_DEV), 1)
    norms_ref[...] = jnp.sum(jnp.where(eye_row == eye_col, own_norm, 0.0), axis=0, keepdims=True)

    def near_step(c):
        r = c * CROWS
        got(("far", c, 1))
        near_out_r[c, 0:HROWS] = (part_r[r : r + HROWS] + far_l[c].astype(jnp.float32)).astype(jnp.bfloat16)
        near_out_r[c, HROWS:CROWS] = part_r[r + HROWS : r + CROWS].astype(jnp.bfloat16)
        send(("near", c, 1), near_out_r.at[c], near_in_l.at[c], at(dy=1))
        got(("far", c, 3))
        near_out_l[c, 0:HROWS] = part_l[r : r + HROWS].astype(jnp.bfloat16)
        near_out_l[c, HROWS:CROWS] = (part_l[r + HROWS : r + CROWS] + far_r[c].astype(jnp.float32)).astype(jnp.bfloat16)
        send(("near", c, 3), near_out_l.at[c], near_in_r.at[c], at(dy=3))

    def relay_second(half, k):
        for side, part, ds in ((1, 0, 3), (3, 1, 1)):
            got(("second", half, k, side))
            block = piece(half, k, ds, part)
            send(("third", half, k, side), block, block, device(half, 0, side))
            sibling(half, k, ds)

    def finish_second(half, k):
        for side in (1, 3):
            got(("third", half, k, side))
        sibling(half, k, 2)

    def logits_of(pair, shifts):
        for dz in shifts:
            for dx in range(4):
                got(("sib", 0, dx, dz, None))
                got(("sib", 1, dz, dx, None))
        rows = pl.ds(pl.multiple_of(pair * PAIR, PAIR), PAIR)
        out = lax.dot_general(
            hw_ref[...], gathered[rows, :], (((1,), (1,)), ((), ())), preferred_element_type=jnp.float32
        )
        logits_ref[:, rows] = out
        mx[0, pl.ds(pair, 1), :] = jnp.max(out, axis=0, keepdims=True)

    project(0, part_own)
    for side, part, df in ((1, 0, 3), (3, 1, 1)):
        for half in (0, 1):
            got(("first", half, side))
            block = piece(half, df, 0, part)
            send(("relay", half, side), block, block, device(half, side, 0))
    for half in (0, 1):
        spread(half, 3)
        spread(half, 1)
    for half in (0, 1):
        sibling(half, 3, 0)
        sibling(half, 1, 0)
    near_step(0)
    for half in (0, 1):
        for side in (1, 3):
            got(("relay", half, side))
        spread(half, 2)
    for half in (0, 1):
        relay_second(half, 0)
    for half in (0, 1):
        sibling(half, 2, 0)
    near_step(1)
    for k in (3, 1):
        for half in (0, 1):
            relay_second(half, k)
    near_step(2)
    for half in (0, 1):
        finish_second(half, 0)
    for half in (0, 1):
        relay_second(half, 2)
    near_step(3)
    for k in (3, 1):
        for half in (0, 1):
            finish_second(half, k)
    mine, other = z // 2, 1 - z // 2

    for half in (0, 1):
        finish_second(half, 2)
    logits_of(mine, (0, 1, 3))
    logits_of(other, (2,))

    def spread_max(stage, moves):
        for i, move in enumerate(moves):
            send(("max", stage, i), mx.at[stage], mx_in.at[stage, i], at(**move))

    def take_max(stage, moves):
        m = mx[stage]
        for i in range(len(moves)):
            got(("max", stage, i))
            m = jnp.maximum(m, mx_in[stage, i])
        return m

    spread_max(0, plane)
    mx[1] = take_max(0, plane)
    spread_max(1, column)

    for c in range(CHUNKS):
        r = slice(c * CROWS, (c + 1) * CROWS)
        got(("near", c, 1))
        got(("near", c, 3))
        total = tok_v[r].astype(jnp.float32) + part_own[r] + near_in_l[c].astype(jnp.float32)
        states_ref[r] = (total + near_in_r[c].astype(jnp.float32)).astype(jnp.bfloat16)
    top = take_max(1, column)
    for i in range(4):
        h = HD * (i % 2)
        max_ref[i : i + 1, :] = top[i // 2 : i // 2 + 1, h : h + HD]
    for c in copies.values():
        c.wait_send()


def tail_call(attention, gain, tokens, w_out, head_t):
    vmem = pl.BlockSpec(memory_space=pltpu.VMEM)
    hbm = pl.BlockSpec(memory_space=pltpu.HBM)
    half = jnp.bfloat16
    return pl.pallas_call(
        tail_kernel,
        out_shape=(
            jax.ShapeDtypeStruct((ROWS, WIDTH), half),
            jax.ShapeDtypeStruct((1, REQ_DEV), jnp.float32),
            jax.ShapeDtypeStruct((4, HD), jnp.float32),
            jax.ShapeDtypeStruct((VLOC, 2 * PAIR), jnp.float32),
        ),
        in_specs=[vmem, vmem, hbm, vmem, vmem],
        out_specs=(vmem, vmem, vmem, vmem),
        scratch_shapes=[
            pltpu.VMEM((ROWS, WIDTH), half),
            pltpu.VMEM((REQ_DEV, D), half),
            pltpu.VMEM((2 * PAIR, D), half),
            pltpu.VMEM((3, REQ_DEV, WIDTH), half),
            pltpu.VMEM((3, REQ_DEV, WIDTH), half),
            pltpu.VMEM((ROWS, WIDTH), half),
            pltpu.VMEM((CHUNKS, HROWS, WIDTH), half),
            pltpu.VMEM((CHUNKS, HROWS, WIDTH), half),
            pltpu.VMEM((ROWS, WIDTH), jnp.float32),
            pltpu.VMEM((ROWS, WIDTH), jnp.float32),
            pltpu.VMEM((ROWS, WIDTH), jnp.float32),
            pltpu.VMEM((CHUNKS, CROWS, WIDTH), half),
            pltpu.VMEM((CHUNKS, CROWS, WIDTH), half),
            pltpu.VMEM((CHUNKS, CROWS, WIDTH), half),
            pltpu.VMEM((CHUNKS, CROWS, WIDTH), half),
            pltpu.VMEM((2, 2, PAIR), jnp.float32),
            pltpu.VMEM((2, 15, 2, PAIR), jnp.float32),
            pltpu.SemaphoreType.DMA,
            pltpu.SemaphoreType.DMA((N_COPIES,)),
            pltpu.SemaphoreType.DMA((N_COPIES,)),
        ],
        compiler_params=pltpu.CompilerParams(
            vmem_limit_bytes=28 * 1024 * 1024, collective_id=0, has_side_effects=True
        ),
        name="tail",
    )(attention, gain.reshape(1, D), in_hbm(tokens), w_out, head_t)


def out_kernel(*refs):
    n = len(refs) // 2
    sems = refs[-1]
    moves = [pltpu.make_async_copy(refs[i], refs[n + i], sems.at[i]) for i in range(n)]
    for m in moves:
        m.start()
    for m in moves:
        m.wait()


def out_call(*arrays):
    return pl.pallas_call(
        out_kernel,
        out_shape=tuple(jax.ShapeDtypeStruct(a.shape, a.dtype) for a in arrays),
        in_specs=[pl.BlockSpec(memory_space=pltpu.VMEM)] * len(arrays),
        out_specs=tuple(pl.BlockSpec(memory_space=pltpu.HBM) for _ in arrays),
        scratch_shapes=[pltpu.SemaphoreType.DMA((len(arrays),))],
        compiler_params=pltpu.CompilerParams(vmem_limit_bytes=4 * 1024 * 1024),
        name="write",
    )(*arrays)


def local(
    tokens,
    w_query,
    query_bias,
    w_keyval,
    keyval_bias,
    w_out,
    attn_gain,
    final_norm_gain,
    head_weight,
    kv_pool,
    cache_len,
):
    new_kv, attention, w_out_v, head_v = attention_call(
        cache_len,
        tokens,
        w_query,
        w_keyval,
        query_bias,
        keyval_bias,
        attn_gain,
        kv_pool.reshape(POOL, KW),
        w_out,
        head_weight.T,
    )
    states, norms, top, logits_t = out_call(*tail_call(attention, final_norm_gain, tokens, w_out_v, head_v))
    return (
        states,
        new_kv.reshape(ROWS, 1, KW),
        norms.reshape(REQ_DEV),
        top.reshape(2 * PAIR),
        logits_t.T,
    )


def solution(mesh):
    return jax.shard_map(
        local,
        mesh=mesh,
        in_specs=(
            P("req", None),
            P(None, "tp"),
            P("tp"),
            P(None, "tp"),
            P("tp"),
            P("tp", None),
            P(),
            P(),
            P(None, ("req", "tp")),
            P("req", "tp", None),
            P(),
        ),
        out_specs=(P("req", "tp"), P("req", "tp", None), P("req"), P(), P(None, ("req", "tp"))),
        check_vma=False,
    )
```
